32 devices in a mesh: dp: 4 (over y, x), region: 8 (over z, core).
Axes of the slice: x: 2, y: 2, z: 4, core: 2. Of those that a mesh axis runs over, the one named last changes fastest.
Arguments:
- features: bfloat16 [4, 8, 16, 16, 16, 128], P('dp', 'region'), may hold values from -6 to 6
- conv_weight: bfloat16 [3, 3, 3, 128, 128], replicated, may hold values from -0.109375 to 0.109375
- down_weight: bfloat16 [2, 2, 2, 128, 128], replicated, may hold values from -0.1875 to 0.1875
- coarse_cotangent: bfloat16 [4, 8, 16, 16, 16, 128], P('dp', 'region'), may hold values from -6 to 6
- brick_coords: int32 [4, 8, 3], P('dp', 'region'), may hold values from 0 to 7, as said below
- neighbours: int32 [4, 8, 26], P('dp', 'region'), may hold values from -1 to 7, as said below
- parents: int32 [4, 8], P('dp', 'region'), may hold values from 0 to 7, as said below
Outputs:
- coarse_features: bfloat16 [4, 8, 16, 16, 16, 128], P('dp', 'region')
- input_grad: bfloat16 [4, 8, 16, 16, 16, 128], P('dp', 'region')
- conv_grad: float32 [3, 3, 3, 128, 128], replicated
- down_grad: float32 [2, 2, 2, 128, 128], replicated
The draws below stay inside these ranges and needn't reach their ends.
Inputs may be any that keep to these rules, and one draw needn't show every extreme that they name: `brick_coords`: slot s lies on region index s; its first coordinate is s, the second below 4, the third below 2; the coordinates of one scene's slots are distinct. `neighbours`: entry d names the slot whose coordinates are the brick's own plus offset d, or -1 where no slot has them; named slots lie on the same or an adjacent region index, and the relation is symmetric. `parents`: the parent is 2 (x // 2) + (y // 2) of the brick's coordinates; coarse brick c lies on region index c.
All inputs are finite; a program needn't handle non-finite values.
Results may differ from the reference program's by a relative error of at most 0.005.
Values may be sent and summed in bfloat16 or wider, within the bound.
A program may use at most 192 MiB of HBM per device.

```python
import jax
import jax.numpy as jnp
import numpy as np
from jax import lax

CHANNELS = 128
BRICK = 16
BRICK_DEV = 1
GRID_Y = 4
GRID_Z = 2
SCENES = 4
TOTAL_BRICKS = 8
COARSE = 8
N_REGION = 8


OFFSET_TABLE = np.array([(a, b, c) for a in (-1, 0, 1) for b in (-1, 0, 1) for c in (-1, 0, 1) if (a, b, c) != (0, 0, 0)], dtype=np.int32)


def brick_layout(key):
    keys = jax.random.split(jax.random.fold_in(key, 7), SCENES * N_REGION)
    places = jax.vmap(lambda single: jax.random.permutation(single, GRID_Y * GRID_Z))(keys)[:, :BRICK_DEV]
    places = places.reshape(SCENES, TOTAL_BRICKS).astype(jnp.int32)
    first = jnp.broadcast_to((jnp.arange(TOTAL_BRICKS, dtype=jnp.int32) // BRICK_DEV)[None, :], (SCENES, TOTAL_BRICKS))
    return jnp.stack([first, places // GRID_Z, places % GRID_Z], axis=-1).astype(jnp.int32)


def draw_brick_coords(key, part):
    return brick_layout(key)


def draw_neighbours(key, part):
    coords = brick_layout(key)
    wanted = coords[:, :, None, :] + jnp.asarray(OFFSET_TABLE)[None, None, :, :]
    matches = jnp.all(wanted[:, :, :, None, :] == coords[:, None, None, :, :], axis=-1).astype(jnp.int32)
    labels = jnp.arange(1, TOTAL_BRICKS + 1, dtype=jnp.int32)
    return (jnp.sum(matches * labels, axis=-1) - 1).astype(jnp.int32)


def draw_parents(key, part):
    coords = brick_layout(key)
    return (2 * (coords[:, :, 0] // 2) + coords[:, :, 1] // 2).astype(jnp.int32)


def block_levels(key, extent, cuts, least, high):
    factor_of, own = 1.0, jax.random.fold_in(key, 6)
    for position, shards_of in cuts:
        heights = jnp.exp(jax.random.uniform(jax.random.fold_in(own, position), (shards_of,), jnp.float32, least / len(cuts), high / len(cuts)))
        factor_of = factor_of * jnp.repeat(heights, extent[position] // shards_of).reshape([-1 if axis == position else 1 for axis in range(len(extent))])
    return factor_of


def centred(own_key, shape, deviation, reach, cuts=(), held_as=jnp.bfloat16):
    values = jax.random.normal(own_key, shape, jnp.float32) * deviation
    if len(cuts) > 0:
        values = block_levels(own_key, shape, cuts, -0.22, 0.18) * values
    return jnp.clip(values, min=-reach, max=reach).astype(held_as)


def setup_inputs(seed: int = 0) -> dict:
    key_of = jax.random.split(jax.random.key(seed), 8)
    return {
        "features": centred(key_of[0], (SCENES, TOTAL_BRICKS, BRICK, BRICK, BRICK, CHANNELS), 1.0, 6.0, ((0, 4), (1, 8))),
        "conv_weight": centred(key_of[1], (3, 3, 3, CHANNELS, CHANNELS), (27 * CHANNELS) ** -0.5, 0.109375),
        "down_weight": centred(key_of[2], (2, 2, 2, CHANNELS, CHANNELS), (8 * CHANNELS) ** -0.5, 0.1875),
        "coarse_cotangent": centred(key_of[3], (SCENES, COARSE, BRICK, BRICK, BRICK, CHANNELS), 1.0, 6.0, ((0, 4), (1, 8))),
        "brick_coords": draw_brick_coords(jax.random.fold_in(key_of[7], 71), 0),
        "neighbours": draw_neighbours(jax.random.fold_in(key_of[7], 71), 0),
        "parents": draw_parents(jax.random.fold_in(key_of[7], 71), 0),
    }


OFFSETS = [(a, b, c) for a in (-1, 0, 1) for b in (-1, 0, 1) for c in (-1, 0, 1) if (a, b, c) != (0, 0, 0)]
loss_scale = 1024.0


def source_cut(offset, brick_edge):
    if offset < 0:
        return slice(brick_edge - 1, brick_edge)
    if offset == 0:
        return slice(0, brick_edge)
    return slice(0, 1)


def pad_bricks(center, fetcher, present):
    pieces = {}
    for number, (a, b, c) in enumerate(OFFSETS):
        section = fetcher(number, a, b, c)
        keeper = present[:, number].reshape(-1, 1, 1, 1, 1)
        pieces[(a, b, c)] = jnp.where(keeper, section, jnp.zeros_like(section))
    pieces[(0, 0, 0)] = center
    slabs = []
    for a in (-1, 0, 1):
        rows = []
        for b in (-1, 0, 1):
            rows.append(jnp.concatenate([pieces[(a, b, c)] for c in (-1, 0, 1)], axis=3))
        slabs.append(jnp.concatenate(rows, axis=2))
    return jnp.concatenate(slabs, axis=1)


def tap_windows(padded, a):
    brick_edge, channels = padded.shape[1] - 2, padded.shape[-1]
    parts = [padded[:, a:a + brick_edge, b:b + brick_edge, c:c + brick_edge] for b in range(3) for c in range(3)]
    return jnp.concatenate(parts, axis=-1).reshape(-1, 9 * channels)


def conv_bricks(padded, kernel):
    brick_count, brick_edge, channels = padded.shape[0], padded.shape[1] - 2, padded.shape[-1]
    summed = jnp.zeros((brick_count * brick_edge ** 3, kernel.shape[-1]), jnp.float32)
    for a in range(3):
        window = tap_windows(padded, a)
        summed = summed + jnp.dot(window, kernel[a].reshape(9 * channels, -1), preferred_element_type=jnp.float32)
    return summed.reshape(brick_count, brick_edge, brick_edge, brick_edge, -1)


def kernel_grads(padded, grads):
    channels = padded.shape[-1]
    flat_grads = grads.reshape(-1, grads.shape[-1])
    result = []
    for a in range(3):
        window = tap_windows(padded, a)
        result.append(lax.dot_general(window, flat_grads, (((0,), (0,)), ((), ())), preferred_element_type=jnp.float32).reshape(3, 3, channels, -1))
    return jnp.stack(result)


def padded_scene(field, neighbours):
    brick_edge = field.shape[1]
    present = neighbours >= 0
    indices = jnp.where(present, neighbours, 0).astype(jnp.int32)

    def fetcher(number, a, b, c):
        return field[:, source_cut(a, brick_edge), source_cut(b, brick_edge), source_cut(c, brick_edge)][indices[:, number]]

    return pad_bricks(field, fetcher, present)


def reference(features, conv_weight, down_weight, coarse_cotangent, brick_coords, neighbours, parents):
    brick_edge, channels = features.shape[2], features.shape[-1]
    half_edge = brick_edge // 2
    brick_count = features.shape[1]
    coarse_count = coarse_cotangent.shape[1]
    flipped = jnp.swapaxes(jnp.flip(conv_weight, (0, 1, 2)), 3, 4)
    conv_total = jnp.zeros((3, 3, 3, channels, channels), jnp.float32)
    down_total = jnp.zeros((2, 2, 2, channels, channels), jnp.float32)
    coarse_list = []
    grad_list = []
    for scene in range(features.shape[0]):
        field = features[scene]
        padded = padded_scene(field, neighbours[scene])
        outputs = (conv_bricks(padded, conv_weight) + field.astype(jnp.float32)).astype(jnp.bfloat16)
        fine_split = outputs.reshape(brick_count, half_edge, 2, half_edge, 2, half_edge, 2, channels).astype(jnp.float32)
        blocks = jnp.einsum("bixjykzc,xyzcd->bijkd", fine_split, down_weight.astype(jnp.float32)).astype(jnp.bfloat16)
        coords = brick_coords[scene]
        octant = (coords[:, 0] % 2) * 4 + (coords[:, 1] % 2) * 2 + coords[:, 2] % 2
        targets = (parents[scene] * 8 + octant).astype(jnp.int32)
        coarse = jnp.zeros((coarse_count * 8, half_edge, half_edge, half_edge, channels), jnp.float32)
        coarse = coarse.at[targets].add(blocks.astype(jnp.float32))
        coarse = coarse.reshape(coarse_count, 2, 2, 2, half_edge, half_edge, half_edge, channels)
        coarse = coarse.transpose(0, 1, 4, 2, 5, 3, 6, 7).reshape(coarse_count, brick_edge, brick_edge, brick_edge, channels)
        coarse_list.append(coarse.astype(jnp.bfloat16))
        cotangent = coarse_cotangent[scene].reshape(coarse_count, 2, half_edge, 2, half_edge, 2, half_edge, channels)
        cotangent = cotangent.transpose(0, 1, 3, 5, 2, 4, 6, 7).reshape(coarse_count * 8, half_edge, half_edge, half_edge, channels)
        chosen = cotangent[targets]
        grad_outputs = jnp.einsum("bijkd,xyzcd->bixjykzc", chosen.astype(jnp.float32), down_weight.astype(jnp.float32))
        grad_outputs = grad_outputs.reshape(brick_count, brick_edge, brick_edge, brick_edge, channels).astype(jnp.bfloat16)
        down_total = down_total + jnp.einsum("bixjykzc,bijkd->xyzcd", fine_split, chosen.astype(jnp.float32))
        padded_back = padded_scene(grad_outputs, neighbours[scene])
        input_grad = grad_outputs.astype(jnp.float32) + conv_bricks(padded_back, flipped)
        grad_list.append(input_grad.astype(jnp.bfloat16))
        conv_total = conv_total + kernel_grads(padded, grad_outputs)
    return (jnp.stack(coarse_list), jnp.stack(grad_list), conv_total / loss_scale, down_total / loss_scale)
```

```python
import functools

import jax
import jax.numpy as jnp
from jax import lax
from jax.experimental import pallas as pl
from jax.experimental.pallas import tpu as pltpu
from jax.sharding import PartitionSpec as P

loss_scale = 1024.0
MESH = pl.DeviceIdType.MESH
F32, BF16 = jnp.float32, jnp.bfloat16


def nn(a, b):
    return lax.dot_general(a, b, (((1,), (0,)), ((), ())), preferred_element_type=F32)


def nt(a, b):
    return lax.dot_general(a, b, (((1,), (1,)), ((), ())), preferred_element_type=F32)


def shifted(s, low, mid, high):
    edge = s.shape[-2]
    axis = s.ndim - 2
    row = lax.broadcasted_iota(jnp.int32, s.shape, axis)
    first = pltpu.roll(s, 1, axis) * jnp.where(row == 0, low, mid)
    last = pltpu.roll(s, edge - 1, axis) * jnp.where(row == edge - 1, high, mid)
    return first, s * mid, last


def put_plane(dst, x, even, odd, low, mid, high):
    half, c = even.shape[0], even.shape[-1]
    for k, v in enumerate(shifted(even, low, mid, high)):
        dst[x, 0:half, :, 2 * k * c + c : 2 * k * c + 2 * c] = v.astype(BF16)
    for k, v in enumerate(shifted(odd, low, mid, high)):
        dst[x, 1 : half + 1, :, 2 * k * c : 2 * k * c + c] = v.astype(BF16)


def put_row(dst, x, y, row, low, mid, high):
    c = row.shape[-1]
    for k, v in enumerate(shifted(row, low, mid, high)):
        at = 2 * k * c + (y % 2) * c
        dst[x, y // 2, :, at : at + c] = v.astype(BF16)


def masks(nb, a):
    def m(b, c):
        i = (a + 1) * 9 + (b + 1) * 3 + (c + 1)
        i = i - 1 if i > 13 else i
        return jnp.where(nb[i] >= 0, 1.0, 0.0).astype(F32)

    return {b: (m(b, -1), m(b, 0), m(b, 1)) for b in (-1, 0, 1)}


def put_halo(dst, x, even, odd, mask):
    half, edge = even.shape[0], dst.shape[0]
    put_plane(dst, x, even, odd, *mask[0])
    put_row(dst, x, 0, odd[half - 1], *mask[-1])
    put_row(dst, x, edge - 1, even[0], *mask[1])


def zero_rows(dst, edge, c):
    z = jnp.zeros((edge, dst.shape[2], c), BF16)
    for k in range(3):
        dst[1 : edge + 1, 0, :, 2 * k * c : 2 * k * c + c] = z
        dst[1 : edge + 1, edge // 2, :, 2 * k * c + c : 2 * k * c + 2 * c] = z


def tap_of(s, pin, pout):
    b = 2 * s + pin - pout
    return b if 0 <= b <= 2 else None


class Reduction:
    def __init__(self, env, acc, start, n, refs):
        self.env, self.acc, self.start, self.n = env, acc, start, n
        self.to_plane, self.from_plane, self.by_z, self.gathered, self.send, self.recv = refs
        self.p = n // env.plane
        self.wait = None

    def go(self, stage, src, dst, peers):
        send, recv = self.send.at[stage], self.recv.at[stage]
        for k, to in enumerate(peers, 1):
            self.env.send(src(k), dst.at[k], send, recv, to)
        self.wait = (dst.at[pl.ds(1, len(peers))], send, recv)

    def land(self):
        size, send, recv = self.wait
        copy = pltpu.make_async_remote_copy(
            src_ref=size, dst_ref=size, send_sem=send, recv_sem=recv,
            device_id=self.env.mate, device_id_type=MESH,
        )
        copy.wait()

    def step(self, stage):
        env, p = self.env, self.p
        if stage > 0:
            self.land()
        if stage == 0:
            self.to_plane[...] = self.acc[pl.ds(self.start, self.n)].astype(BF16)
            self.go(
                0,
                lambda k: self.to_plane.at[rows_at(env.rank_at(k) * p, p)],
                self.from_plane,
                env.plane_peers,
            )
        elif stage == 1:
            part = self.acc[rows_at(self.start + env.rank * p, p)]
            for k in range(1, env.plane):
                part += self.from_plane[k].astype(F32)
            self.by_z[0] = part.astype(BF16)
            self.go(1, lambda k: self.by_z.at[0], self.by_z, env.z_peers)
        elif stage == 2:
            part = self.by_z[env.z].astype(F32)
            for z in range(1, env.zs):
                part += self.by_z[lax.rem(env.z - z + env.zs, env.zs)].astype(F32)
            self.gathered[0] = part.astype(BF16)
            self.go(2, lambda k: self.gathered.at[0], self.gathered, env.plane_peers)

    def unpack(self, out, at):
        self.land()
        env, p = self.env, self.p
        for k in range(env.plane):
            row = lax.rem(env.rank - k + env.plane, env.plane) * p
            out[rows_at(at + row, p)] = self.gathered[k].astype(F32)


def reduction_scratch(n, plane, zs, c):
    p = n // plane
    return [
        pltpu.VMEM((n, c), BF16),
        pltpu.VMEM((plane, p, c), BF16),
        pltpu.VMEM((zs, p, c), BF16),
        pltpu.VMEM((plane, p, c), BF16),
        pltpu.SemaphoreType.DMA((3,)),
        pltpu.SemaphoreType.DMA((3,)),
    ]


REDUCTION_REFS = 6


def rows_at(start, n):
    return pl.ds(pl.multiple_of(start, 16) if not isinstance(start, int) else start, n)


class Peers:
    def __init__(self, dps, zs):
        self.zs = zs
        self.plane = 2 * dps
        n = 2 * zs
        self.dp, self.region = lax.axis_index("dp"), lax.axis_index("region")
        self.core, self.z = lax.rem(self.region, 2), lax.div(self.region, 2)
        self.rank = self.dp * 2 + self.core
        self.mate = (self.dp, self.region + 1 - 2 * self.core)
        self.right = (self.dp, lax.rem(self.region + 1, n))
        self.left = (self.dp, lax.rem(self.region + n - 1, n))
        self.plane_peers = [self.device(self.rank_at(k)) for k in range(1, self.plane)]
        self.z_peers = [
            (self.dp, 2 * lax.rem(self.z + k, zs) + self.core) for k in range(1, zs)
        ]
        self.peers = [self.right, self.left] + self.plane_peers + self.z_peers

    def rank_at(self, k):
        return lax.rem(self.rank + k, self.plane)

    def device(self, rank):
        return (lax.div(rank, 2), 2 * self.z + lax.rem(rank, 2))

    def greet(self):
        barrier = pltpu.get_barrier_semaphore()
        for peer in self.peers:
            pl.semaphore_signal(barrier, inc=1, device_id=peer, device_id_type=MESH)

    def met(self):
        pl.semaphore_wait(pltpu.get_barrier_semaphore(), len(self.peers))

    def send(self, src, dst, send, recv, to):
        copy = pltpu.make_async_remote_copy(
            src_ref=src, dst_ref=dst, send_sem=send, recv_sem=recv,
            device_id=to, device_id_type=MESH,
        )
        copy.start()
        return copy


def start(src, dst, sem):
    copy = pltpu.make_async_copy(src, dst, sem)
    copy.start()
    return copy


def kernel(
    sizes, nb_hbm, xyz_hbm, parent, f_hbm, cot, cw_hbm, dw_hbm,
    coarse_out, ig, conv_out, down_out,
    f, cw, dw, field, wide, gfold, up, outf, gt, tt, acc,
    flo, fhi, cot1, cot2, tag, tag2, ch, clo, chi, blocks, blocks2, nb, xyz, sends, recvs, loads, *refs
):
    dps, zs, cuts, conv_rows, down_rows = sizes
    env = Peers(dps, zs)
    edge, c = f.shape[0], f.shape[-1]
    half = edge // 2
    rows = half * edge
    n = REDUCTION_REFS
    live = {}
    at = 0
    for k, size in enumerate(cuts + (down_rows,)):
        if size:
            j = len(live)
            live[k] = Reduction(env, acc, at, size, refs[n * j : n * j + n])
        at += size
    down_at = len(cuts)

    def advance(k, stage):
        if k in live:
            live[k].step(stage)

    def send(i, src, dst, to):
        return env.send(src, dst, sends.at[i], recvs.at[i], to)

    env.greet()
    small = (nb_hbm, nb), (xyz_hbm, xyz)
    small_copies = [start(a, b, loads.at[i]) for i, (a, b) in enumerate(small)]
    step = 4
    laps = edge // step
    parts = [pl.ds(i * step, step) for i in range(laps)]
    f_copies = [start(f_hbm.at[p], f.at[p], loads.at[2 + i]) for i, p in enumerate(parts)]
    cw_copy = start(cw_hbm, cw, loads.at[laps + 2])
    mine_at = pl.ds(env.core * half, half)
    cot1_copy = start(cot.at[mine_at], cot1, loads.at[laps + 3])
    dw_copy = start(dw_hbm, dw, loads.at[laps + 4])

    for copy in small_copies:
        copy.wait()
    quad = lax.rem(xyz[1], 2) * 2 + lax.rem(xyz[2], 2)
    octant = env.core * 4 + quad
    tag[...] = jnp.full(tag.shape, parent[0] * 8 + octant, jnp.int32)

    def window(x, m, a, s):
        return field[pl.ds(x + a, m), s : s + half].reshape(m * rows, 6 * c)

    def lhs(x, m):
        return jnp.concatenate([window(x, m, a, s) for a in range(3) for s in range(2)], -1)

    below, above = masks(nb, -1), masks(nb, 1)
    zero_rows(field, edge, c)

    for i, copy in enumerate(f_copies):
        copy.wait()

        @pl.loop(i * step, (i + 1) * step)
        def _(x):
            put_plane(
                field, x + 1, f[x, :, 0].astype(F32), f[x, :, 1].astype(F32), 0.0, 1.0, 0.0
            )

    zero = jnp.zeros((c, c), BF16)

    def weights(block):
        for a in range(3):
            for s in range(2):
                for k in range(3):
                    for pin in range(2):
                        at = ((2 * a + s) * 3 + k) * 2 * c + pin * c
                        for pout in range(2):
                            b = tap_of(s, pin, pout)
                            wide[at : at + c, pout * c : (pout + 1) * c] = (
                                zero if b is None else block(a, b, k)
                            )

    cw_copy.wait()
    weights(lambda a, b, k: cw[9 * a + 3 * b + k])
    origin = lax.div(env.dp, dps)

    def forward(m, to, scale=1):
        @pl.loop(origin + m, origin + to)
        def _(i):
            x = i * (step * scale)
            out = nn(lhs(x, step), wide[...]).reshape(step, half, edge, 2 * c)
            for q in range(2):
                outf[q, pl.ds(x, step)] = (
                    (out[..., q * c : (q + 1) * c] + f[pl.ds(x, step), :, q].astype(F32))
                    .astype(BF16)
                    .astype(F32)
                )

    middle = laps // 2
    forward(1, middle)
    env.met()
    theirs_at = pl.ds((1 - env.core) * half, half)
    cot_copy = send(0, cot.at[theirs_at], cot2, env.mate)
    tag_copy = send(1, tag, tag2, env.mate)
    up_copy = send(2, f.at[edge - 1], flo, env.right)
    down_copy = send(3, f.at[0], fhi, env.left)
    forward(middle, laps - 1)

    cot1_copy.wait()
    dw_copy.wait()
    cot_copy.wait()
    tag_copy.wait()
    home = parent[0] == env.region
    picked = jnp.zeros((half, half, half, c), F32)
    for y in range(2):
        at = (slice(None), slice(y * half, (y + 1) * half))
        both = jnp.where(home, cot1[at].astype(F32), cot2[at].astype(F32))
        for z in range(2):
            picked = jnp.where(quad == 2 * y + z, both[:, :, z * half : (z + 1) * half], picked)
    ch[...] = picked.astype(BF16)
    clo_copy = send(4, ch.at[half - 1], clo, env.right)
    chi_copy = send(5, ch.at[0], chi, env.left)

    up[...] = jnp.zeros_like(up)

    def lift(v):
        m = v.shape[0] * v.shape[1]
        v = v.astype(F32).reshape(m, half, c)
        for r in range(2):
            up[r, 0:m, pl.ds(r, half, 2), :] = v
        both = [up[r, 0:m].reshape(m * edge, c).astype(BF16) for r in range(2)]
        return jnp.concatenate(both, -1)

    def dwt(p):
        return jnp.concatenate(
            [jnp.concatenate([dw[4 * p + 2 * q + r] for r in range(2)], -1) for q in range(2)], 0
        )

    raised = lift(picked)
    for p in range(2):
        g = nt(raised, dwt(p)).astype(BF16).reshape(half, half, edge, 2 * c)
        for i in range(half):
            gfold[2 * i + p] = g[i]

    up_copy.wait()
    down_copy.wait()
    put_halo(field, 0, flo[:, 0].astype(F32), flo[:, 1].astype(F32), below)
    put_halo(field, edge + 1, fhi[:, 0].astype(F32), fhi[:, 1].astype(F32), above)

    flat = gfold[...].reshape(edge * rows, 2 * c)
    gt[...] = flat.astype(F32).T.astype(BF16)
    if conv_rows > 27 * c:
        acc[27 * c : conv_rows] = jnp.zeros((conv_rows - 27 * c, c), F32)
    if down_rows > 8 * c:
        acc[conv_rows + 8 * c :] = jnp.zeros((down_rows - 8 * c, c), F32)
    for a in range(3):
        for s in range(2):
            tt[s] = nn(gt[...], window(0, edge, a, s))
        for b in range(3):
            for k in range(3):
                total = jnp.zeros((c, c), F32)
                for s in range(2):
                    for pin in range(2):
                        for pout in range(2):
                            if tap_of(s, pin, pout) == b:
                                at = (2 * k + pin) * c
                                total += tt[s, pout * c : (pout + 1) * c, at : at + c]
                tap = 9 * a + 3 * b + k
                acc[tap * c : (tap + 1) * c] = total.T * (1.0 / loss_scale)
        advance(a, 0)

    forward(0, 1, laps - 1)
    advance(0, 1)
    forward(1, 2, laps - 1)
    advance(1, 1)

    taken = []
    for p in range(2):
        for r in range(2):
            halves = []
            for q in range(2):
                pieces = [
                    outf[q, 2 * i + p, :, pl.ds(r, half, 2), :].reshape(half * half, c)
                    for i in range(half)
                ]
                halves.append(jnp.concatenate(pieces, 0).astype(BF16))
            taken.append(jnp.concatenate(halves, -1))
    cht = ch[...].reshape(half**3, c).astype(F32).T.astype(BF16)
    for p in range(2):
        for r in range(2):
            d = nn(cht, taken[2 * p + r])
            for q in range(2):
                at = conv_rows + (4 * p + 2 * q + r) * c
                acc[at : at + c] = d[:, q * c : (q + 1) * c].T * (1.0 / loss_scale)
    advance(down_at, 0)
    dwf = jnp.concatenate(
        [dw[4 * p + 2 * q + r] for p in range(2) for r in range(2) for q in range(2)], 0
    )
    blocks[...] = nn(jnp.concatenate(taken, -1), dwf).astype(BF16).reshape(blocks.shape)
    blocks_copy = send(6, blocks, blocks2, env.mate)

    clo_copy.wait()
    chi_copy.wait()
    for edge_of, p, x, mask in ((clo, 1, 0, below), (chi, 0, edge + 1, above)):
        g = nt(lift(edge_of[...][None]), dwt(p)).astype(BF16).astype(F32)
        g = g.reshape(half, edge, 2 * c)
        put_halo(field, x, g[..., :c], g[..., c:], mask)

    @pl.loop(0, edge)
    def _(x):
        g = gfold[x].astype(F32)
        put_plane(field, x + 1, g[..., :c], g[..., c:], 0.0, 1.0, 0.0)

    advance(2, 1)
    weights(lambda a, b, k: cw[9 * (2 - a) + 3 * (2 - b) + 2 - k].T)
    advance(0, 2)

    def backward(m, to):
        @pl.loop(origin + m, origin + to)
        def _(i):
            x = i * step
            out = nn(lhs(x, step), wide[...]).reshape(step, half, edge, 2 * c)
            out = (out + gfold[pl.ds(x, step)].astype(F32)).astype(BF16)
            for q in range(2):
                ig[pl.ds(x, step), :, q] = out[..., q * c : (q + 1) * c]

    quarter = laps // 4
    backward(0, quarter)
    advance(down_at, 1)
    advance(1, 2)
    backward(quarter, 2 * quarter)
    advance(2, 2)
    backward(2 * quarter, 3 * quarter)
    advance(down_at, 2)
    backward(3 * quarter, laps)

    blocks_copy.wait()
    mine, theirs = blocks[...].astype(F32), blocks2[...].astype(F32)
    own_tag, other_tag = tag[0:1, :], tag2[0:1, :]
    for x in range(2):
        for y in range(2):
            pair = []
            for z in range(2):
                here = env.region * 8 + 4 * x + 2 * y + z
                ours = jnp.where(own_tag == here, 1.0, 0.0).astype(F32)
                others = jnp.where(other_tag == here, 1.0, 0.0).astype(F32)
                pair.append(mine * ours + theirs * others)
            coarse_out[x * half : (x + 1) * half, y * half : (y + 1) * half] = jnp.concatenate(
                pair, 2
            ).astype(BF16)
    for k, one in live.items():
        if k == down_at:
            one.unpack(down_out, 0)
        else:
            one.unpack(conv_out, one.start)


def finish(*refs):
    n = len(refs) // 2
    ins, outs, sems = refs[:n], refs[n : 2 * n], refs[2 * n]
    copies = [
        start(ins[i].at[pl.ds(0, outs[i].shape[0])], outs[i], sems.at[i]) for i in range(n)
    ]
    for copy in copies:
        copy.wait()


def local(features, conv_weight, down_weight, coarse_cotangent, brick_coords, neighbours, parents):
    edge, c = features.shape[2], features.shape[-1]
    half = edge // 2
    dps, regions = lax.axis_size("dp"), lax.axis_size("region")
    zs = regions // 2
    unit = 32 * dps
    conv_rows = -(-27 * c // unit) * unit
    down_rows = -(-8 * c // unit) * unit
    ends = [9 * c // unit * unit, 18 * c // unit * unit, conv_rows]
    cuts = (ends[0], ends[1] - ends[0], ends[2] - ends[1])
    total = conv_rows + down_rows
    hbm = pl.BlockSpec(memory_space=pl.ANY)
    smem = pl.BlockSpec(memory_space=pltpu.SMEM)
    plane = pltpu.VMEM((half, 2, edge, c), BF16)
    cube = pltpu.VMEM((half, half, half, c), BF16)
    layer = pltpu.VMEM((half, half, c), BF16)
    tags = pltpu.VMEM((8, 128), jnp.int32)
    scratch = [
        pltpu.VMEM((edge, half, 2, edge, c), BF16),
        pltpu.VMEM((27, c, c), BF16),
        pltpu.VMEM((8, c, c), BF16),
        pltpu.VMEM((edge + 2, half + 1, edge, 6 * c), BF16),
        pltpu.VMEM((36 * c, 2 * c), BF16),
        pltpu.VMEM((edge, half, edge, 2 * c), BF16),
        pltpu.VMEM((2, half * half, edge, c), F32),
        pltpu.VMEM((2, edge, half, edge, c), F32),
        pltpu.VMEM((2 * c, edge * half * edge), BF16),
        pltpu.VMEM((2, 2 * c, 6 * c), F32),
        pltpu.VMEM((total, c), F32),
        plane,
        plane,
        pltpu.VMEM((half, edge, edge, c), BF16),
        pltpu.VMEM((half, edge, edge, c), BF16),
        tags,
        tags,
        cube,
        layer,
        layer,
        cube,
        cube,
        pltpu.SMEM((26,), jnp.int32),
        pltpu.SMEM((3,), jnp.int32),
        pltpu.SemaphoreType.DMA((7,)),
        pltpu.SemaphoreType.DMA((7,)),
        pltpu.SemaphoreType.DMA((edge // 4 + 5,)),
    ]
    for n in cuts + (down_rows,):
        if n:
            scratch += reduction_scratch(n, 2 * dps, zs, c)
    def shapes(conv_n, down_n):
        return (
            jax.ShapeDtypeStruct((edge, edge, edge, c), BF16),
            jax.ShapeDtypeStruct((edge, half, 2, edge, c), BF16),
            jax.ShapeDtypeStruct((conv_n, c), F32),
            jax.ShapeDtypeStruct((down_n, c), F32),
        )

    parts = pl.pallas_call(
        functools.partial(kernel, (dps, zs, cuts, conv_rows, down_rows)),
        out_shape=shapes(conv_rows, down_rows),
        in_specs=[hbm] * 2 + [smem] + [hbm] * 4,
        out_specs=(pl.BlockSpec(memory_space=pltpu.VMEM),) * 4,
        scratch_shapes=scratch,
        compiler_params=pltpu.CompilerParams(
            collective_id=0, has_side_effects=True, vmem_limit_bytes=40 * 1024 * 1024
        ),
    )(
        pltpu.with_memory_space_constraint(neighbours.reshape(26), pltpu.HBM),
        pltpu.with_memory_space_constraint(brick_coords.reshape(3), pltpu.HBM),
        parents.reshape(1),
        *(
            pltpu.with_memory_space_constraint(v, pltpu.HBM)
            for v in (
                features.reshape(edge, half, 2, edge, c),
                coarse_cotangent.reshape(edge, edge, edge, c),
                conv_weight.reshape(27, c, c),
                down_weight.reshape(8, c, c),
            )
        ),
    )
    coarse, ig, conv_total, down_total = pl.pallas_call(
        finish,
        out_shape=shapes(27 * c, 8 * c),
        in_specs=[hbm] * 4,
        out_specs=(hbm,) * 4,
        scratch_shapes=[pltpu.SemaphoreType.DMA((4,))],
        compiler_params=pltpu.CompilerParams(vmem_limit_bytes=4 * 1024 * 1024),
    )(*parts)
    return (
        coarse.reshape(1, 1, edge, edge, edge, c),
        ig.reshape(1, 1, edge, edge, edge, c),
        conv_total.reshape(3, 3, 3, c, c),
        down_total.reshape(2, 2, 2, c, c),
    )


def solution(mesh):
    in_specs = (
        P("dp", "region", None, None, None, None),
        P(),
        P(),
        P("dp", "region", None, None, None, None),
        P("dp", "region", None),
        P("dp", "region", None),
        P("dp", "region"),
    )
    out_specs = (
        P("dp", "region", None, None, None, None),
        P("dp", "region", None, None, None, None),
        P(),
        P(),
    )
    return jax.shard_map(local, mesh=mesh, in_specs=in_specs, out_specs=out_specs, check_vma=False)
```

```python
import functools

import jax
import jax.numpy as jnp
from jax import lax
from jax.experimental import pallas as pl
from jax.experimental.pallas import tpu as pltpu
from jax.sharding import PartitionSpec as P

loss_scale = 1024.0
MESH = pl.DeviceIdType.MESH
F32, BF16 = jnp.float32, jnp.bfloat16
PIECES = 4


def nn(a, b):
    return lax.dot_general(a, b, (((1,), (0,)), ((), ())), preferred_element_type=F32)


def nt(a, b):
    return lax.dot_general(a, b, (((1,), (1,)), ((), ())), preferred_element_type=F32)


def shifted(s, low, mid, high):
    edge = s.shape[-2]
    axis = s.ndim - 2
    row = lax.broadcasted_iota(jnp.int32, s.shape, axis)
    first = pltpu.roll(s, 1, axis) * jnp.where(row == 0, low, mid)
    last = pltpu.roll(s, edge - 1, axis) * jnp.where(row == edge - 1, high, mid)
    return first, s * mid, last


def put_plane(dst, x, even, odd, low, mid, high):
    half, c = even.shape[0], even.shape[-1]
    for k, v in enumerate(shifted(even, low, mid, high)):
        dst[x, 0:half, :, 2 * k * c + c : 2 * k * c + 2 * c] = v.astype(BF16)
    for k, v in enumerate(shifted(odd, low, mid, high)):
        dst[x, 1 : half + 1, :, 2 * k * c : 2 * k * c + c] = v.astype(BF16)


def put_row(dst, x, y, row, low, mid, high):
    c = row.shape[-1]
    for k, v in enumerate(shifted(row, low, mid, high)):
        at = 2 * k * c + (y % 2) * c
        dst[x, y // 2, :, at : at + c] = v.astype(BF16)


def masks(nb, a):
    def m(b, c):
        i = (a + 1) * 9 + (b + 1) * 3 + (c + 1)
        i = i - 1 if i > 13 else i
        return jnp.where(nb[i] >= 0, 1.0, 0.0).astype(F32)

    return {b: (m(b, -1), m(b, 0), m(b, 1)) for b in (-1, 0, 1)}


def put_halo(dst, x, even, odd, mask):
    half, edge = even.shape[0], dst.shape[0]
    put_plane(dst, x, even, odd, *mask[0])
    put_row(dst, x, 0, odd[half - 1], *mask[-1])
    put_row(dst, x, edge - 1, even[0], *mask[1])


def zero_rows(dst, edge, c):
    z = jnp.zeros((edge, dst.shape[2], c), BF16)
    for k in range(3):
        dst[1 : edge + 1, 0, :, 2 * k * c : 2 * k * c + c] = z
        dst[1 : edge + 1, edge // 2, :, 2 * k * c + c : 2 * k * c + 2 * c] = z


def tap_of(s, pin, pout):
    b = 2 * s + pin - pout
    return b if 0 <= b <= 2 else None


class Reduction:
    def __init__(self, env, acc, whole, start, n, split, refs):
        self.env, self.acc, self.whole, self.start, self.n = env, acc, whole, start, n
        self.to_core, self.from_core, self.to_dp, self.from_dp = refs[:4]
        self.by_z, self.gathered, self.send, self.recv = refs[4:8]
        self.h = n // 2
        self.p = self.h // env.dps
        self.half = start + env.core * self.h
        self.piece = self.half + env.dp * self.p
        self.split = split
        if split:
            self.to_z, self.z_all = refs[8:]
            self.s = self.p // env.zs
        middle = (self.z_reduce, self.z_gather) if split else (self.z_exchange,)
        self.steps = (self.core_reduce, self.dp_reduce) + middle + (self.dp_gather, self.core_gather)
        self.stage = 0
        self.wait = None

    def go(self, src, dst, peers):
        send, recv = self.send.at[self.stage], self.recv.at[self.stage]
        for k, to in enumerate(peers, 1):
            self.env.send(src(k), dst.at[k], send, recv, to)
        self.wait = (dst.at[pl.ds(1, len(peers))], send, recv)

    def swap(self, src, dst):
        send, recv = self.send.at[self.stage], self.recv.at[self.stage]
        self.env.send(src, dst, send, recv, self.env.mate)
        self.wait = (dst, send, recv)

    def land(self):
        size, send, recv = self.wait
        copy = pltpu.make_async_remote_copy(
            src_ref=size, dst_ref=size, send_sem=send, recv_sem=recv,
            device_id=self.env.mate, device_id_type=MESH,
        )
        copy.wait()

    def step(self):
        if self.stage > 0:
            self.land()
        if self.stage < len(self.steps):
            self.steps[self.stage]()
        self.stage += 1

    def done(self):
        return self.stage > len(self.steps)

    def core_reduce(self):
        other = self.start + (1 - self.env.core) * self.h
        self.to_core[...] = self.acc[rows_at(other, self.h)].astype(BF16)
        self.swap(self.to_core, self.from_core)

    def dp_reduce(self):
        env, p = self.env, self.p
        part = self.acc[rows_at(self.half, self.h)] + self.from_core[...].astype(F32)
        self.acc[rows_at(self.half, self.h)] = part
        self.to_dp[...] = part.astype(BF16)
        self.go(lambda k: self.to_dp.at[rows_at(env.dp_at(k) * p, p)], self.from_dp, env.dp_peers)

    def plane_sum(self):
        part = self.acc[rows_at(self.piece, self.p)]
        for k in range(1, self.env.dps):
            part += self.from_dp[k].astype(F32)
        return part

    def z_exchange(self):
        self.by_z[0] = self.plane_sum().astype(BF16)
        self.go(lambda k: self.by_z.at[0], self.by_z, self.env.z_peers)

    def z_reduce(self):
        env, s = self.env, self.s
        part = self.plane_sum()
        self.acc[rows_at(self.piece, self.p)] = part
        self.to_z[...] = part.astype(BF16)
        self.go(lambda k: self.to_z.at[rows_at(env.z_at(k) * s, s)], self.by_z, env.z_peers)

    def z_gather(self):
        env = self.env
        part = self.acc[rows_at(self.piece + env.z * self.s, self.s)]
        for k in range(1, env.zs):
            part += self.by_z[k].astype(F32)
        self.z_all[0] = part.astype(BF16)
        self.go(lambda k: self.z_all.at[0], self.z_all, env.z_peers)

    def dp_gather(self):
        env = self.env
        if self.split:
            for k in range(env.zs):
                row = lax.rem(env.z - k + env.zs, env.zs) * self.s
                self.gathered[0, rows_at(row, self.s)] = self.z_all[k]
        else:
            part = self.by_z[env.z].astype(F32)
            for z in range(1, env.zs):
                part += self.by_z[lax.rem(env.z - z + env.zs, env.zs)].astype(F32)
            self.gathered[0] = part.astype(BF16)
        self.go(lambda k: self.gathered.at[0], self.gathered, env.dp_peers)

    def core_gather(self):
        env, p = self.env, self.p
        for k in range(env.dps):
            row = lax.rem(env.dp - k + env.dps, env.dps) * p
            self.whole[rows_at(self.half + row, p)] = self.gathered[k]
        ref = self.whole.at[rows_at(self.half, self.h)]
        self.swap(ref, ref)


def reduction_scratch(n, split, dps, zs, c):
    h = n // 2
    p = h // dps
    s = p // zs if split else p
    stages = 6 if split else 5
    out = [
        pltpu.VMEM((h, c), BF16),
        pltpu.VMEM((h, c), BF16),
        pltpu.VMEM((h, c), BF16),
        pltpu.VMEM((dps, p, c), BF16),
        pltpu.VMEM((zs, s, c), BF16),
        pltpu.VMEM((dps, p, c), BF16),
        pltpu.SemaphoreType.DMA((stages,)),
        pltpu.SemaphoreType.DMA((stages,)),
    ]
    if split:
        out += [pltpu.VMEM((p, c), BF16), pltpu.VMEM((zs, s, c), BF16)]
    return out


def rows_at(start, n):
    return pl.ds(pl.multiple_of(start, 16) if not isinstance(start, int) else start, n)


class Peers:
    def __init__(self, dps, zs):
        self.dps, self.zs = dps, zs
        n = 2 * zs
        self.dp, self.region = lax.axis_index("dp"), lax.axis_index("region")
        self.core, self.z = lax.rem(self.region, 2), lax.div(self.region, 2)
        self.mate = (self.dp, self.region + 1 - 2 * self.core)
        self.right = (self.dp, lax.rem(self.region + 1, n))
        self.left = (self.dp, lax.rem(self.region + n - 1, n))
        self.dp_peers = [(self.dp_at(k), self.region) for k in range(1, dps)]
        self.z_peers = [(self.dp, 2 * self.z_at(k) + self.core) for k in range(1, zs)]
        self.peers = [self.mate, self.right, self.left] + self.dp_peers + self.z_peers

    def dp_at(self, k):
        return lax.rem(self.dp + k, self.dps)

    def z_at(self, k):
        return lax.rem(self.z + k, self.zs)

    def greet(self):
        barrier = pltpu.get_barrier_semaphore()
        for peer in self.peers:
            pl.semaphore_signal(barrier, inc=1, device_id=peer, device_id_type=MESH)

    def met(self):
        pl.semaphore_wait(pltpu.get_barrier_semaphore(), len(self.peers))

    def send(self, src, dst, send, recv, to):
        copy = pltpu.make_async_remote_copy(
            src_ref=src, dst_ref=dst, send_sem=send, recv_sem=recv,
            device_id=to, device_id_type=MESH,
        )
        copy.start()
        return copy


def start(src, dst, sem):
    copy = pltpu.make_async_copy(src, dst, sem)
    copy.start()
    return copy


def kernel(
    sizes, nb_hbm, xyz_hbm, parent, f_hbm, cot, cw_hbm, dw_hbm,
    coarse_out, ig, conv_out, down_out,
    f, cw, dw, field, wide, gfold, up, outf, gt, tt, acc, whole,
    flo, fhi, cot1, cot2, tag, tag2, ch, clo, chi, blocks, blocks2, nb, xyz, sends, recvs, loads, *refs
):
    dps, zs, cuts, conv_rows, down_rows = sizes
    env = Peers(dps, zs)
    edge, c = f.shape[0], f.shape[-1]
    half = edge // 2
    rows = half * edge
    live = {}
    at = used = 0
    for k, (size, split) in enumerate(cuts):
        if size:
            count = 10 if split else 8
            live[k] = Reduction(env, acc, whole, at, size, split, refs[used : used + count])
            used += count
        at += size
    down_at = len(cuts) - 1

    def advance(*which):
        for k in which:
            if k in live and not live[k].done():
                live[k].step()

    def send(i, src, dst, to):
        return env.send(src, dst, sends.at[i], recvs.at[i], to)

    env.greet()
    small = (nb_hbm, nb), (xyz_hbm, xyz)
    small_copies = [start(a, b, loads.at[i]) for i, (a, b) in enumerate(small)]
    step = 4
    laps = edge // step
    parts = [pl.ds(i * step, step) for i in range(laps)]
    f_copies = [start(f_hbm.at[p], f.at[p], loads.at[2 + i]) for i, p in enumerate(parts)]
    cw_copy = start(cw_hbm, cw, loads.at[laps + 2])
    mine_at = pl.ds(env.core * half, half)
    cot1_copy = start(cot.at[mine_at], cot1, loads.at[laps + 3])
    dw_copy = start(dw_hbm, dw, loads.at[laps + 4])

    def window(x, m, a, s):
        return field[pl.ds(x + a, m), s : s + half].reshape(m * rows, 6 * c)

    def lhs(x, m):
        return jnp.concatenate([window(x, m, a, s) for a in range(3) for s in range(2)], -1)

    zero_rows(field, edge, c)

    for i, copy in enumerate(f_copies):
        copy.wait()

        @pl.loop(i * step, (i + 1) * step)
        def _(x):
            put_plane(
                field, x + 1, f[x, :, 0].astype(F32), f[x, :, 1].astype(F32), 0.0, 1.0, 0.0
            )

    env.met()
    theirs_at = pl.ds((1 - env.core) * half, half)
    last = 2 * zs - 1

    def shift(i, src, dst, to, leaves, comes):
        copy = pltpu.make_async_remote_copy(
            src_ref=src, dst_ref=dst, send_sem=sends.at[i], recv_sem=recvs.at[i],
            device_id=to, device_id_type=MESH,
        )

        @pl.when(leaves)
        def _():
            copy.start()

        @pl.when(jnp.logical_not(comes))
        def _():
            dst[...] = jnp.zeros_like(dst)

        return copy, leaves, comes

    def settle(copy, leaves, comes):
        @pl.when(leaves)
        def _():
            copy.wait_send()

        @pl.when(comes)
        def _():
            copy.wait_recv()

    has_right, has_left = env.region < last, env.region > 0
    up_copy = shift(2, f.at[edge - 1], flo, env.right, has_right, has_left)
    down_copy = shift(3, f.at[0], fhi, env.left, has_left, has_right)
    cot_copy = send(0, cot.at[theirs_at], cot2, env.mate)

    zero = jnp.zeros((c, c), BF16)

    def weights(block):
        for a in range(3):
            for s in range(2):
                for k in range(3):
                    for pin in range(2):
                        at = ((2 * a + s) * 3 + k) * 2 * c + pin * c
                        for pout in range(2):
                            b = tap_of(s, pin, pout)
                            wide[at : at + c, pout * c : (pout + 1) * c] = (
                                zero if b is None else block(a, b, k)
                            )

    cw_copy.wait()
    weights(lambda a, b, k: cw[9 * a + 3 * b + k])
    origin = lax.div(env.dp, dps)

    def forward(m, to, scale=1):
        @pl.loop(origin + m, origin + to)
        def _(i):
            x = i * (step * scale)
            out = nn(lhs(x, step), wide[...]).reshape(step, half, edge, 2 * c)
            for q in range(2):
                outf[q, pl.ds(x, step)] = (
                    (out[..., q * c : (q + 1) * c] + f[pl.ds(x, step), :, q].astype(F32))
                    .astype(BF16)
                    .astype(F32)
                )

    forward(1, laps // 2)

    for copy in small_copies:
        copy.wait()
    quad = lax.rem(xyz[1], 2) * 2 + lax.rem(xyz[2], 2)
    octant = env.core * 4 + quad
    tag[...] = jnp.full(tag.shape, parent[0, 0] * 8 + octant, jnp.int32)
    tag_copy = send(1, tag, tag2, env.mate)
    below, above = masks(nb, -1), masks(nb, 1)

    cot1_copy.wait()
    dw_copy.wait()
    cot_copy.wait()
    home = parent[0, 0] == env.region
    picked = jnp.zeros((half, half, half, c), F32)
    for y in range(2):
        at = (slice(None), slice(y * half, (y + 1) * half))
        both = jnp.where(home, cot1[at].astype(F32), cot2[at].astype(F32))
        for z in range(2):
            picked = jnp.where(quad == 2 * y + z, both[:, :, z * half : (z + 1) * half], picked)
    ch[...] = picked.astype(BF16)
    clo_copy = shift(4, ch.at[half - 1], clo, env.right, has_right, has_left)
    chi_copy = shift(5, ch.at[0], chi, env.left, has_left, has_right)

    up[...] = jnp.zeros_like(up)

    def lift(v):
        m = v.shape[0] * v.shape[1]
        v = v.astype(F32).reshape(m, half, c)
        for r in range(2):
            up[r, 0:m, pl.ds(r, half, 2), :] = v
        both = [up[r, 0:m].reshape(m * edge, c).astype(BF16) for r in range(2)]
        return jnp.concatenate(both, -1)

    def dwt(p):
        return jnp.concatenate(
            [jnp.concatenate([dw[4 * p + 2 * q + r] for r in range(2)], -1) for q in range(2)], 0
        )

    raised = lift(picked)
    for p in range(2):
        g = nt(raised, dwt(p)).astype(BF16).reshape(half, half, edge, 2 * c)
        for i in range(half):
            gfold[2 * i + p] = g[i]

    settle(*up_copy)
    settle(*down_copy)
    put_halo(field, 0, flo[:, 0].astype(F32), flo[:, 1].astype(F32), below)
    put_halo(field, edge + 1, fhi[:, 0].astype(F32), fhi[:, 1].astype(F32), above)

    flat = gfold[...].reshape(edge * rows, 2 * c)
    gt[...] = flat.astype(F32).T.astype(BF16)
    if conv_rows > 27 * c:
        acc[27 * c : conv_rows] = jnp.zeros((conv_rows - 27 * c, c), F32)
    if down_rows > 8 * c:
        acc[conv_rows + 8 * c :] = jnp.zeros((down_rows - 8 * c, c), F32)
    def gradient(a):
        for s in range(2):
            tt[s] = nn(gt[...], window(0, edge, a, s))
        for b in range(3):
            for k in range(3):
                total = jnp.zeros((c, c), F32)
                for s in range(2):
                    for pin in range(2):
                        for pout in range(2):
                            if tap_of(s, pin, pout) == b:
                                at = (2 * k + pin) * c
                                total += tt[s, pout * c : (pout + 1) * c, at : at + c]
                tap = 9 * a + 3 * b + k
                acc[tap * c : (tap + 1) * c] = total.T * (1.0 / loss_scale)

    gradient(0)
    advance(0)
    gradient(1)
    advance(1, 0)
    gradient(2)
    advance(2, 1)
    forward(laps // 2, laps - 1)
    advance(0, 2)
    forward(0, 1, laps - 1)
    advance(1)
    forward(1, 2, laps - 1)
    advance(0)

    taken = []
    for p in range(2):
        for r in range(2):
            halves = []
            for q in range(2):
                pieces = [
                    outf[q, 2 * i + p, :, pl.ds(r, half, 2), :].reshape(half * half, c)
                    for i in range(half)
                ]
                halves.append(jnp.concatenate(pieces, 0).astype(BF16))
            taken.append(jnp.concatenate(halves, -1))
    cht = ch[...].reshape(half**3, c).astype(F32).T.astype(BF16)
    for p in range(2):
        for r in range(2):
            d = nn(cht, taken[2 * p + r])
            for q in range(2):
                at = conv_rows + (4 * p + 2 * q + r) * c
                acc[at : at + c] = d[:, q * c : (q + 1) * c].T * (1.0 / loss_scale)
    advance(down_at, 2)
    dwf = jnp.concatenate(
        [dw[4 * p + 2 * q + r] for p in range(2) for r in range(2) for q in range(2)], 0
    )
    blocks[...] = nn(jnp.concatenate(taken, -1), dwf).astype(BF16).reshape(blocks.shape)
    blocks_copy = send(6, blocks, blocks2, env.mate)

    settle(*clo_copy)
    settle(*chi_copy)
    for edge_of, p, x, mask in ((clo, 1, 0, below), (chi, 0, edge + 1, above)):
        g = nt(lift(edge_of[...][None]), dwt(p)).astype(BF16).astype(F32)
        g = g.reshape(half, edge, 2 * c)
        put_halo(field, x, g[..., :c], g[..., c:], mask)
    advance(down_at, 1)

    @pl.loop(0, edge)
    def _(x):
        g = gfold[x].astype(F32)
        put_plane(field, x + 1, g[..., :c], g[..., c:], 0.0, 1.0, 0.0)

    weights(lambda a, b, k: cw[9 * (2 - a) + 3 * (2 - b) + 2 - k].T)
    advance(2)

    def backward(m, to):
        @pl.loop(origin + m, origin + to)
        def _(i):
            x = i * step
            out = nn(lhs(x, step), wide[...]).reshape(step, half, edge, 2 * c)
            out = (out + gfold[pl.ds(x, step)].astype(F32)).astype(BF16)
            for q in range(2):
                ig[pl.ds(x, step), :, q] = out[..., q * c : (q + 1) * c]

    quarter = laps // 4
    backward(0, quarter)
    advance(down_at, 0, 1)
    backward(quarter, 2 * quarter)
    advance(2)
    backward(2 * quarter, 3 * quarter)
    advance(down_at, 0, 1)
    backward(3 * quarter, laps)
    advance(2)

    tag_copy.wait()
    blocks_copy.wait()
    mine, theirs = blocks[...].astype(F32), blocks2[...].astype(F32)
    own_tag, other_tag = tag[0:1, :], tag2[0:1, :]
    for x in range(2):
        for y in range(2):
            pair = []
            for z in range(2):
                here = env.region * 8 + 4 * x + 2 * y + z
                ours = jnp.where(own_tag == here, 1.0, 0.0).astype(F32)
                others = jnp.where(other_tag == here, 1.0, 0.0).astype(F32)
                pair.append(mine * ours + theirs * others)
            coarse_out[x * half : (x + 1) * half, y * half : (y + 1) * half] = jnp.concatenate(
                pair, 2
            ).astype(BF16)
    def finish_chunk(k):
        one = live[k]
        while not one.done():
            one.step()
        rows = min(one.start + one.n, 27 * c)
        if k != down_at:
            conv_out[one.start : rows] = whole[one.start : rows].astype(F32)

    advance(down_at, 2)
    for k in (0, 1, 2, down_at):
        if k in live:
            finish_chunk(k)
    down_out[...] = whole[conv_rows : conv_rows + 8 * c].astype(F32)


def finish(*refs):
    n = len(refs) // 2
    sems = refs[2 * n]
    copies = []
    for i in range(n):
        m = refs[i].shape[0] // PIECES
        for k in range(PIECES):
            part = pl.ds(k * m, m)
            sem = sems.at[len(copies)]
            copies.append(start(refs[i].at[part], refs[n + i].at[part], sem))
    for copy in copies:
        copy.wait()


def local(features, conv_weight, down_weight, coarse_cotangent, brick_coords, neighbours, parents):
    edge, c = features.shape[2], features.shape[-1]
    half = edge // 2
    dps, regions = lax.axis_size("dp"), lax.axis_size("region")
    zs = regions // 2
    unit, wide = 32 * dps, 32 * dps * zs
    conv_rows = -(-27 * c // wide) * wide
    down_rows = -(-8 * c // unit) * unit
    ends = [0, 9 * c // wide * wide, 18 * c // wide * wide, conv_rows]
    cuts = tuple((ends[i + 1] - ends[i], True) for i in range(3)) + ((down_rows, False),)
    total = conv_rows + down_rows
    hbm = pl.BlockSpec(memory_space=pl.ANY)
    smem = pl.BlockSpec(memory_space=pltpu.SMEM)
    plane = pltpu.VMEM((half, 2, edge, c), BF16)
    cube = pltpu.VMEM((half, half, half, c), BF16)
    layer = pltpu.VMEM((half, half, c), BF16)
    tags = pltpu.VMEM((8, 128), jnp.int32)
    scratch = [
        pltpu.VMEM((edge, half, 2, edge, c), BF16),
        pltpu.VMEM((27, c, c), BF16),
        pltpu.VMEM((8, c, c), BF16),
        pltpu.VMEM((edge + 2, half + 1, edge, 6 * c), BF16),
        pltpu.VMEM((36 * c, 2 * c), BF16),
        pltpu.VMEM((edge, half, edge, 2 * c), BF16),
        pltpu.VMEM((2, half * half, edge, c), F32),
        pltpu.VMEM((2, edge, half, edge, c), F32),
        pltpu.VMEM((2 * c, edge * half * edge), BF16),
        pltpu.VMEM((2, 2 * c, 6 * c), F32),
        pltpu.VMEM((total, c), F32),
        pltpu.VMEM((total, c), BF16),
        plane,
        plane,
        pltpu.VMEM((half, edge, edge, c), BF16),
        pltpu.VMEM((half, edge, edge, c), BF16),
        tags,
        tags,
        cube,
        layer,
        layer,
        cube,
        cube,
        pltpu.SMEM((26,), jnp.int32),
        pltpu.SMEM((3,), jnp.int32),
        pltpu.SemaphoreType.DMA((7,)),
        pltpu.SemaphoreType.DMA((7,)),
        pltpu.SemaphoreType.DMA((edge // 4 + 5,)),
    ]
    for n, split in cuts:
        if n:
            scratch += reduction_scratch(n, split, dps, zs, c)
    shapes = (
        jax.ShapeDtypeStruct((edge, edge, edge, c), BF16),
        jax.ShapeDtypeStruct((edge, half, 2, edge, c), BF16),
        jax.ShapeDtypeStruct((27 * c, c), F32),
        jax.ShapeDtypeStruct((8 * c, c), F32),
    )
    parts = pl.pallas_call(
        functools.partial(kernel, (dps, zs, cuts, conv_rows, down_rows)),
        out_shape=shapes,
        in_specs=[hbm] * 2 + [smem] + [hbm] * 4,
        out_specs=(pl.BlockSpec(memory_space=pltpu.VMEM),) * 4,
        scratch_shapes=scratch,
        compiler_params=pltpu.CompilerParams(
            collective_id=0, has_side_effects=True, vmem_limit_bytes=40 * 1024 * 1024
        ),
    )(
        pltpu.with_memory_space_constraint(neighbours.reshape(26), pltpu.HBM),
        pltpu.with_memory_space_constraint(brick_coords.reshape(3), pltpu.HBM),
        parents,
        *(
            pltpu.with_memory_space_constraint(v, pltpu.HBM)
            for v in (
                features.reshape(edge, half, 2, edge, c),
                coarse_cotangent.reshape(edge, edge, edge, c),
                conv_weight.reshape(27, c, c),
                down_weight.reshape(8, c, c),
            )
        ),
    )
    coarse, ig, conv_total, down_total = pl.pallas_call(
        finish,
        out_shape=shapes,
        in_specs=[hbm] * 4,
        out_specs=(hbm,) * 4,
        scratch_shapes=[pltpu.SemaphoreType.DMA((4 * PIECES,))],
        compiler_params=pltpu.CompilerParams(vmem_limit_bytes=4 * 1024 * 1024),
    )(*parts)
    return (
        coarse.reshape(1, 1, edge, edge, edge, c),
        ig.reshape(1, 1, edge, edge, edge, c),
        conv_total.reshape(3, 3, 3, c, c),
        down_total.reshape(2, 2, 2, c, c),
    )


def solution(mesh):
    in_specs = (
        P("dp", "region", None, None, None, None),
        P(),
        P(),
        P("dp", "region", None, None, None, None),
        P("dp", "region", None),
        P("dp", "region", None),
        P("dp", "region"),
    )
    out_specs = (
        P("dp", "region", None, None, None, None),
        P("dp", "region", None, None, None, None),
        P(),
        P(),
    )
    return jax.shard_map(local, mesh=mesh, in_specs=in_specs, out_specs=out_specs, check_vma=False)
```

```python
import functools

import jax
import jax.numpy as jnp
from jax import lax
from jax.experimental import pallas as pl
from jax.experimental.pallas import tpu as pltpu
from jax.sharding import PartitionSpec as P

loss_scale = 1024.0
MESH = pl.DeviceIdType.MESH
F32, BF16 = jnp.float32, jnp.bfloat16
PIECES = 1


def nn(a, b):
    return lax.dot_general(a, b, (((1,), (0,)), ((), ())), preferred_element_type=F32)


def nt(a, b):
    return lax.dot_general(a, b, (((1,), (1,)), ((), ())), preferred_element_type=F32)


def shifted(s, low, mid, high):
    edge = s.shape[-2]
    axis = s.ndim - 2
    row = lax.broadcasted_iota(jnp.int32, s.shape, axis)
    first = pltpu.roll(s, 1, axis) * jnp.where(row == 0, low, mid)
    last = pltpu.roll(s, edge - 1, axis) * jnp.where(row == edge - 1, high, mid)
    return first, s * mid, last


def put_plane(dst, x, even, odd, low, mid, high):
    half, c = even.shape[0], even.shape[-1]
    for k, v in enumerate(shifted(even, low, mid, high)):
        dst[x, 0:half, :, 2 * k * c + c : 2 * k * c + 2 * c] = v.astype(BF16)
    for k, v in enumerate(shifted(odd, low, mid, high)):
        dst[x, 1 : half + 1, :, 2 * k * c : 2 * k * c + c] = v.astype(BF16)


def put_row(dst, x, y, row, low, mid, high):
    c = row.shape[-1]
    for k, v in enumerate(shifted(row, low, mid, high)):
        at = 2 * k * c + (y % 2) * c
        dst[x, y // 2, :, at : at + c] = v.astype(BF16)


def masks(nb, a):
    def m(b, c):
        i = (a + 1) * 9 + (b + 1) * 3 + (c + 1)
        i = i - 1 if i > 13 else i
        return jnp.where(nb[i] >= 0, 1.0, 0.0).astype(F32)

    return {b: (m(b, -1), m(b, 0), m(b, 1)) for b in (-1, 0, 1)}


def put_halo(dst, x, even, odd, mask):
    half, edge = even.shape[0], dst.shape[0]
    put_plane(dst, x, even, odd, *mask[0])
    put_row(dst, x, 0, odd[half - 1], *mask[-1])
    put_row(dst, x, edge - 1, even[0], *mask[1])


def zero_rows(dst, edge, c):
    z = jnp.zeros((edge, dst.shape[2], c), BF16)
    for k in range(3):
        dst[1 : edge + 1, 0, :, 2 * k * c : 2 * k * c + c] = z
        dst[1 : edge + 1, edge // 2, :, 2 * k * c + c : 2 * k * c + 2 * c] = z


def tap_of(s, pin, pout):
    b = 2 * s + pin - pout
    return b if 0 <= b <= 2 else None


class Reduction:
    def __init__(self, env, acc, whole, start, n, split, refs):
        self.env, self.acc, self.whole, self.start, self.n = env, acc, whole, start, n
        self.send, self.recv, self.by_z, self.gathered = refs[:4]
        self.h = n // 2
        self.p = self.h // env.dps
        self.half = start + env.core * self.h
        self.piece = self.half + env.dp * self.p
        self.split = split
        if split:
            self.to_core, self.from_core, self.to_dp, self.parts, self.to_z, self.z_all = refs[4:]
            self.s = self.p // env.zs
            steps = (self.core_reduce, self.dp_reduce, self.z_reduce, self.z_gather)
        else:
            self.to_plane, self.parts = refs[4:]
            steps = (self.plane_reduce, self.z_exchange)
        self.steps = steps + (self.dp_gather, self.core_gather)
        self.stage = 0
        self.wait = None

    def go(self, src, dst, peers):
        send, recv = self.send.at[0], self.recv.at[self.stage]
        for k, to in enumerate(peers, 1):
            self.env.send(src(k), dst.at[k], send, recv, to)
        self.wait = (dst.at[pl.ds(1, len(peers))], send, recv)

    def swap(self, src, dst):
        send, recv = self.send.at[0], self.recv.at[self.stage]
        self.env.send(src, dst, send, recv, self.env.mate)
        self.wait = (dst, send, recv)

    def land(self):
        size, send, recv = self.wait
        copy = pltpu.make_async_remote_copy(
            src_ref=size, dst_ref=size, send_sem=send, recv_sem=recv,
            device_id=self.env.mate, device_id_type=MESH,
        )
        copy.wait()

    def step(self):
        if self.stage > 0:
            self.land()
        if self.stage < len(self.steps):
            self.steps[self.stage]()
        self.stage += 1

    def done(self):
        return self.stage > len(self.steps)

    def core_reduce(self):
        other = self.start + (1 - self.env.core) * self.h
        self.to_core[...] = self.acc[rows_at(other, self.h)].astype(BF16)
        self.swap(self.to_core, self.from_core)

    def dp_reduce(self):
        env, p = self.env, self.p
        part = self.acc[rows_at(self.half, self.h)] + self.from_core[...].astype(F32)
        self.acc[rows_at(self.half, self.h)] = part
        self.to_dp[...] = part.astype(BF16)
        self.go(lambda k: self.to_dp.at[rows_at(env.dp_at(k) * p, p)], self.parts, env.dp_peers)

    def plane_sum(self):
        part = self.acc[rows_at(self.piece, self.p)]
        for k in range(1, self.parts.shape[0]):
            part += self.parts[k].astype(F32)
        return part

    def plane_reduce(self):
        env, h, p = self.env, self.h, self.p
        self.to_plane[...] = self.acc[pl.ds(self.start, self.n)].astype(BF16)

        def piece(k):
            dp, core = env.plane_at(k)
            return self.to_plane.at[rows_at(core * h + dp * p, p)]

        self.go(piece, self.parts, env.plane_peers)

    def z_exchange(self):
        self.by_z[0] = self.plane_sum().astype(BF16)
        self.go(lambda k: self.by_z.at[0], self.by_z, self.env.z_peers)

    def z_reduce(self):
        env, s = self.env, self.s
        part = self.plane_sum()
        self.acc[rows_at(self.piece, self.p)] = part
        self.to_z[...] = part.astype(BF16)
        self.go(lambda k: self.to_z.at[rows_at(env.z_at(k) * s, s)], self.by_z, env.z_peers)

    def z_gather(self):
        env = self.env
        part = self.acc[rows_at(self.piece + env.z * self.s, self.s)]
        for k in range(1, env.zs):
            part += self.by_z[k].astype(F32)
        self.z_all[0] = part.astype(BF16)
        self.go(lambda k: self.z_all.at[0], self.z_all, env.z_peers)

    def dp_gather(self):
        env = self.env
        if self.split:
            for k in range(env.zs):
                row = lax.rem(env.z - k + env.zs, env.zs) * self.s
                self.gathered[0, rows_at(row, self.s)] = self.z_all[k]
        else:
            part = self.by_z[env.z].astype(F32)
            for z in range(1, env.zs):
                part += self.by_z[lax.rem(env.z - z + env.zs, env.zs)].astype(F32)
            self.gathered[0] = part.astype(BF16)
        self.go(lambda k: self.gathered.at[0], self.gathered, env.dp_peers)

    def core_gather(self):
        env, p = self.env, self.p
        for k in range(env.dps):
            row = lax.rem(env.dp - k + env.dps, env.dps) * p
            self.whole[rows_at(self.half + row, p)] = self.gathered[k]
        ref = self.whole.at[rows_at(self.half, self.h)]
        self.swap(ref, ref)


def reduction_scratch(n, split, dps, zs, c):
    h = n // 2
    p = h // dps
    s = p // zs if split else p
    out = [
        pltpu.SemaphoreType.DMA((1,)),
        pltpu.SemaphoreType.DMA((6 if split else 4,)),
        pltpu.VMEM((zs, s, c), BF16),
        pltpu.VMEM((dps, p, c), BF16),
    ]
    if split:
        out += [pltpu.VMEM((h, c), BF16)] * 3
        out += [pltpu.VMEM((dps, p, c), BF16)]
        out += [pltpu.VMEM((p, c), BF16), pltpu.VMEM((zs, s, c), BF16)]
    else:
        out += [pltpu.VMEM((n, c), BF16), pltpu.VMEM((2 * dps, p, c), BF16)]
    return out


def rows_at(start, n):
    return pl.ds(pl.multiple_of(start, 16) if not isinstance(start, int) else start, n)


class Peers:
    def __init__(self, dps, zs):
        self.dps, self.zs = dps, zs
        n = 2 * zs
        self.dp, self.region = lax.axis_index("dp"), lax.axis_index("region")
        self.core, self.z = lax.rem(self.region, 2), lax.div(self.region, 2)
        self.mate = (self.dp, self.region + 1 - 2 * self.core)
        self.right = (self.dp, lax.rem(self.region + 1, n))
        self.left = (self.dp, lax.rem(self.region + n - 1, n))
        self.dp_peers = [(self.dp_at(k), self.region) for k in range(1, dps)]
        self.z_peers = [(self.dp, 2 * self.z_at(k) + self.core) for k in range(1, zs)]
        self.plane_peers = []
        for k in range(1, 2 * dps):
            dp, core = self.plane_at(k)
            self.plane_peers.append((dp, 2 * self.z + core))
        self.peers = [self.right, self.left] + self.plane_peers + self.z_peers

    def plane_at(self, k):
        rank = lax.rem(2 * self.dp + self.core + k, 2 * self.dps)
        return lax.div(rank, 2), lax.rem(rank, 2)

    def dp_at(self, k):
        return lax.rem(self.dp + k, self.dps)

    def z_at(self, k):
        return lax.rem(self.z + k, self.zs)

    def greet(self):
        barrier = pltpu.get_barrier_semaphore()
        for peer in self.peers:
            pl.semaphore_signal(barrier, inc=1, device_id=peer, device_id_type=MESH)

    def met(self):
        pl.semaphore_wait(pltpu.get_barrier_semaphore(), len(self.peers))

    def send(self, src, dst, send, recv, to):
        copy = pltpu.make_async_remote_copy(
            src_ref=src, dst_ref=dst, send_sem=send, recv_sem=recv,
            device_id=to, device_id_type=MESH,
        )
        copy.start()
        return copy


def start(src, dst, sem):
    copy = pltpu.make_async_copy(src, dst, sem)
    copy.start()
    return copy


def kernel(
    sizes, nb_hbm, xyz_hbm, parent, f_hbm, cot, cw_hbm, dw_hbm,
    coarse_out, ig, conv_out, down_out,
    f, cw, dw, field, wide, gfold, up, outf, gt, tt, acc, whole,
    flo, fhi, cot1, cot2, tag, tag2, ch, clo, chi, blocks, blocks2, nb, xyz, sends, recvs, loads, *refs
):
    dps, zs, cuts, conv_rows, down_rows = sizes
    env = Peers(dps, zs)
    edge, c = f.shape[0], f.shape[-1]
    half = edge // 2
    rows = half * edge
    live = {}
    at = used = 0
    for k, (size, split) in enumerate(cuts):
        if size:
            count = 10 if split else 6
            live[k] = Reduction(env, acc, whole, at, size, split, refs[used : used + count])
            used += count
        at += size
    down_at = len(cuts) - 1

    def advance(*which):
        for k in which:
            if k in live and not live[k].done():
                live[k].step()

    def send(i, src, dst, to):
        return env.send(src, dst, sends.at[i], recvs.at[i], to)

    step = 4
    laps = edge // step
    parts = [pl.ds(i * step, step) for i in range(laps)]
    f_copies = [start(f_hbm.at[p], f.at[p], loads.at[2 + i]) for i, p in enumerate(parts)]
    env.greet()
    small = (nb_hbm, nb), (xyz_hbm, xyz)
    small_copies = [start(a, b, loads.at[i]) for i, (a, b) in enumerate(small)]
    cw_copy = start(cw_hbm, cw, loads.at[laps + 2])
    mine_at = pl.ds(env.core * half, half)

    def window(x, m, a, s):
        return field[pl.ds(x + a, m), s : s + half].reshape(m * rows, 6 * c)

    def lhs(x, m):
        return jnp.concatenate([window(x, m, a, s) for a in range(3) for s in range(2)], -1)

    zero_rows(field, edge, c)

    for i, copy in enumerate(f_copies):
        copy.wait()
        if i == laps - 1:
            cot1_copy = start(cot.at[mine_at], cot1, loads.at[laps + 3])
            dw_copy = start(dw_hbm, dw, loads.at[laps + 4])

        @pl.loop(i * step, (i + 1) * step)
        def _(x):
            put_plane(
                field, x + 1, f[x, :, 0].astype(F32), f[x, :, 1].astype(F32), 0.0, 1.0, 0.0
            )

    env.met()
    theirs_at = pl.ds((1 - env.core) * half, half)
    last = 2 * zs - 1

    def shift(i, src, dst, to, leaves, comes):
        copy = pltpu.make_async_remote_copy(
            src_ref=src, dst_ref=dst, send_sem=sends.at[i], recv_sem=recvs.at[i],
            device_id=to, device_id_type=MESH,
        )

        @pl.when(leaves)
        def _():
            copy.start()

        @pl.when(jnp.logical_not(comes))
        def _():
            dst[...] = jnp.zeros_like(dst)

        return copy, leaves, comes

    def settle(copy, leaves, comes):
        @pl.when(leaves)
        def _():
            copy.wait_send()

        @pl.when(comes)
        def _():
            copy.wait_recv()

    has_right, has_left = env.region < last, env.region > 0
    up_copy = shift(2, f.at[edge - 1], flo, env.right, has_right, has_left)
    down_copy = shift(3, f.at[0], fhi, env.left, has_left, has_right)
    cot_copy = send(0, cot.at[theirs_at], cot2, env.mate)

    zero = jnp.zeros((c, c), BF16)

    def weights(block):
        for a in range(3):
            for s in range(2):
                for k in range(3):
                    for pin in range(2):
                        at = ((2 * a + s) * 3 + k) * 2 * c + pin * c
                        for pout in range(2):
                            b = tap_of(s, pin, pout)
                            wide[at : at + c, pout * c : (pout + 1) * c] = (
                                zero if b is None else block(a, b, k)
                            )

    cw_copy.wait()
    weights(lambda a, b, k: cw[9 * a + 3 * b + k])
    origin = lax.div(env.dp, dps)

    def forward(m, to, scale=1):
        @pl.loop(origin + m, origin + to)
        def _(i):
            x = i * (step * scale)
            out = nn(lhs(x, step), wide[...]).reshape(step, half, edge, 2 * c)
            for q in range(2):
                outf[q, pl.ds(x, step)] = (
                    (out[..., q * c : (q + 1) * c] + f[pl.ds(x, step), :, q].astype(F32))
                    .astype(BF16)
                    .astype(F32)
                )

    forward(1, laps // 2)

    for copy in small_copies:
        copy.wait()
    quad = lax.rem(xyz[1], 2) * 2 + lax.rem(xyz[2], 2)
    octant = env.core * 4 + quad
    tag[...] = jnp.full(tag.shape, parent[0, 0] * 8 + octant, jnp.int32)
    tag_copy = send(1, tag, tag2, env.mate)
    below, above = masks(nb, -1), masks(nb, 1)

    cot1_copy.wait()
    dw_copy.wait()
    cot_copy.wait()
    home = parent[0, 0] == env.region
    picked = jnp.zeros((half, half, half, c), F32)
    for y in range(2):
        at = (slice(None), slice(y * half, (y + 1) * half))
        both = jnp.where(home, cot1[at].astype(F32), cot2[at].astype(F32))
        for z in range(2):
            picked = jnp.where(quad == 2 * y + z, both[:, :, z * half : (z + 1) * half], picked)
    ch[...] = picked.astype(BF16)
    clo_copy = shift(4, ch.at[half - 1], clo, env.right, has_right, has_left)
    chi_copy = shift(5, ch.at[0], chi, env.left, has_left, has_right)

    up[...] = jnp.zeros_like(up)

    def lift(v):
        m = v.shape[0] * v.shape[1]
        v = v.astype(F32).reshape(m, half, c)
        for r in range(2):
            up[r, 0:m, pl.ds(r, half, 2), :] = v
        both = [up[r, 0:m].reshape(m * edge, c).astype(BF16) for r in range(2)]
        return jnp.concatenate(both, -1)

    def dwt(p):
        return jnp.concatenate(
            [jnp.concatenate([dw[4 * p + 2 * q + r] for r in range(2)], -1) for q in range(2)], 0
        )

    raised = lift(picked)
    for p in range(2):
        g = nt(raised, dwt(p)).astype(BF16).reshape(half, half, edge, 2 * c)
        for i in range(half):
            gfold[2 * i + p] = g[i]

    settle(*up_copy)
    settle(*down_copy)
    put_halo(field, 0, flo[:, 0].astype(F32), flo[:, 1].astype(F32), below)
    put_halo(field, edge + 1, fhi[:, 0].astype(F32), fhi[:, 1].astype(F32), above)

    flat = gfold[...].reshape(edge * rows, 2 * c)
    gt[...] = flat.astype(F32).T.astype(BF16)
    if conv_rows > 27 * c:
        acc[27 * c : conv_rows] = jnp.zeros((conv_rows - 27 * c, c), F32)
    if down_rows > 8 * c:
        acc[conv_rows + 8 * c :] = jnp.zeros((down_rows - 8 * c, c), F32)
    def gradient(a):
        for s in range(2):
            tt[s] = nn(gt[...], window(0, edge, a, s))
        for b in range(3):
            for k in range(3):
                total = jnp.zeros((c, c), F32)
                for s in range(2):
                    for pin in range(2):
                        for pout in range(2):
                            if tap_of(s, pin, pout) == b:
                                at = (2 * k + pin) * c
                                total += tt[s, pout * c : (pout + 1) * c, at : at + c]
                tap = 9 * a + 3 * b + k
                acc[tap * c : (tap + 1) * c] = total.T * (1.0 / loss_scale)

    gradient(0)
    advance(0)
    gradient(1)
    advance(1, 0)
    gradient(2)
    advance(2, 1)
    forward(laps // 2, laps - 1)
    advance(0, 2)
    forward(0, 1, laps - 1)
    advance(1)
    forward(1, 2, laps - 1)
    advance(0)

    taken = []
    for p in range(2):
        for r in range(2):
            halves = []
            for q in range(2):
                pieces = [
                    outf[q, 2 * i + p, :, pl.ds(r, half, 2), :].reshape(half * half, c)
                    for i in range(half)
                ]
                halves.append(jnp.concatenate(pieces, 0).astype(BF16))
            taken.append(jnp.concatenate(halves, -1))
    cht = ch[...].reshape(half**3, c).astype(F32).T.astype(BF16)
    for p in range(2):
        for r in range(2):
            d = nn(cht, taken[2 * p + r])
            for q in range(2):
                at = conv_rows + (4 * p + 2 * q + r) * c
                acc[at : at + c] = d[:, q * c : (q + 1) * c].T * (1.0 / loss_scale)
    advance(down_at, 2)
    dwf = jnp.concatenate(
        [dw[4 * p + 2 * q + r] for p in range(2) for r in range(2) for q in range(2)], 0
    )
    blocks[...] = nn(jnp.concatenate(taken, -1), dwf).astype(BF16).reshape(blocks.shape)
    blocks_copy = send(6, blocks, blocks2, env.mate)

    settle(*clo_copy)
    settle(*chi_copy)
    for edge_of, p, x, mask in ((clo, 1, 0, below), (chi, 0, edge + 1, above)):
        g = nt(lift(edge_of[...][None]), dwt(p)).astype(BF16).astype(F32)
        g = g.reshape(half, edge, 2 * c)
        put_halo(field, x, g[..., :c], g[..., c:], mask)
    advance(1)

    @pl.loop(0, edge)
    def _(x):
        g = gfold[x].astype(F32)
        put_plane(field, x + 1, g[..., :c], g[..., c:], 0.0, 1.0, 0.0)

    weights(lambda a, b, k: cw[9 * (2 - a) + 3 * (2 - b) + 2 - k].T)


    def backward(m, to):
        @pl.loop(origin + m, origin + to)
        def _(i):
            x = i * step
            out = nn(lhs(x, step), wide[...]).reshape(step, half, edge, 2 * c)
            out = (out + gfold[pl.ds(x, step)].astype(F32)).astype(BF16)
            for q in range(2):
                ig[pl.ds(x, step), :, q] = out[..., q * c : (q + 1) * c]

    quarter = laps // 4
    backward(0, quarter)
    advance(2, down_at, 0, 1)
    backward(quarter, 2 * quarter)
    advance(2)
    backward(2 * quarter, 3 * quarter)
    advance(down_at, 0, 1)
    backward(3 * quarter, laps)
    advance(2)

    tag_copy.wait()
    blocks_copy.wait()
    mine, theirs = blocks[...].astype(F32), blocks2[...].astype(F32)
    own_tag, other_tag = tag[0:1, :], tag2[0:1, :]
    for x in range(2):
        for y in range(2):
            pair = []
            for z in range(2):
                here = env.region * 8 + 4 * x + 2 * y + z
                ours = jnp.where(own_tag == here, 1.0, 0.0).astype(F32)
                others = jnp.where(other_tag == here, 1.0, 0.0).astype(F32)
                pair.append(mine * ours + theirs * others)
            coarse_out[x * half : (x + 1) * half, y * half : (y + 1) * half] = jnp.concatenate(
                pair, 2
            ).astype(BF16)
    def finish_chunk(k):
        one = live[k]
        while not one.done():
            one.step()
        rows = min(one.start + one.n, 27 * c)
        if k != down_at:
            conv_out[one.start : rows] = whole[one.start : rows].astype(F32)

    advance(down_at, 2)
    for k in (0, 1, 2, down_at):
        if k in live:
            finish_chunk(k)
    down_out[...] = whole[conv_rows : conv_rows + 8 * c].astype(F32)


def finish(*refs):
    n = len(refs) // 2
    sems = refs[2 * n]
    copies = []
    for i in range(n):
        m = refs[i].shape[0] // PIECES
        for k in range(PIECES):
            part = pl.ds(k * m, m)
            sem = sems.at[len(copies)]
            copies.append(start(refs[i].at[part], refs[n + i].at[part], sem))
    for copy in copies:
        copy.wait()


def local(features, conv_weight, down_weight, coarse_cotangent, brick_coords, neighbours, parents):
    edge, c = features.shape[2], features.shape[-1]
    half = edge // 2
    dps, regions = lax.axis_size("dp"), lax.axis_size("region")
    zs = regions // 2
    unit, wide = 32 * dps, 32 * dps * zs
    conv_rows = -(-27 * c // wide) * wide
    down_rows = -(-8 * c // unit) * unit
    ends = [0, 9 * c // wide * wide, 18 * c // wide * wide, conv_rows]
    cuts = tuple((ends[i + 1] - ends[i], True) for i in range(3)) + ((down_rows, False),)
    total = conv_rows + down_rows
    hbm = pl.BlockSpec(memory_space=pl.ANY)
    smem = pl.BlockSpec(memory_space=pltpu.SMEM)
    plane = pltpu.VMEM((half, 2, edge, c), BF16)
    cube = pltpu.VMEM((half, half, half, c), BF16)
    layer = pltpu.VMEM((half, half, c), BF16)
    tags = pltpu.VMEM((8, 128), jnp.int32)
    scratch = [
        pltpu.VMEM((edge, half, 2, edge, c), BF16),
        pltpu.VMEM((27, c, c), BF16),
        pltpu.VMEM((8, c, c), BF16),
        pltpu.VMEM((edge + 2, half + 1, edge, 6 * c), BF16),
        pltpu.VMEM((36 * c, 2 * c), BF16),
        pltpu.VMEM((edge, half, edge, 2 * c), BF16),
        pltpu.VMEM((2, half * half, edge, c), F32),
        pltpu.VMEM((2, edge, half, edge, c), F32),
        pltpu.VMEM((2 * c, edge * half * edge), BF16),
        pltpu.VMEM((2, 2 * c, 6 * c), F32),
        pltpu.VMEM((total, c), F32),
        pltpu.VMEM((total, c), BF16),
        plane,
        plane,
        pltpu.VMEM((half, edge, edge, c), BF16),
        pltpu.VMEM((half, edge, edge, c), BF16),
        tags,
        tags,
        cube,
        layer,
        layer,
        cube,
        cube,
        pltpu.SMEM((26,), jnp.int32),
        pltpu.SMEM((3,), jnp.int32),
        pltpu.SemaphoreType.DMA((7,)),
        pltpu.SemaphoreType.DMA((7,)),
        pltpu.SemaphoreType.DMA((edge // 4 + 5,)),
    ]
    for n, split in cuts:
        if n:
            scratch += reduction_scratch(n, split, dps, zs, c)
    shapes = (
        jax.ShapeDtypeStruct((edge, edge, edge, c), BF16),
        jax.ShapeDtypeStruct((edge, half, 2, edge, c), BF16),
        jax.ShapeDtypeStruct((27 * c, c), F32),
        jax.ShapeDtypeStruct((8 * c, c), F32),
    )
    parts = pl.pallas_call(
        functools.partial(kernel, (dps, zs, cuts, conv_rows, down_rows)),
        out_shape=shapes,
        in_specs=[hbm] * 2 + [smem] + [hbm] * 4,
        out_specs=(pl.BlockSpec(memory_space=pltpu.VMEM),) * 4,
        scratch_shapes=scratch,
        compiler_params=pltpu.CompilerParams(
            collective_id=0, has_side_effects=True, vmem_limit_bytes=40 * 1024 * 1024
        ),
    )(
        pltpu.with_memory_space_constraint(neighbours.reshape(26), pltpu.HBM),
        pltpu.with_memory_space_constraint(brick_coords.reshape(3), pltpu.HBM),
        parents,
        *(
            pltpu.with_memory_space_constraint(v, pltpu.HBM)
            for v in (
                features.reshape(edge, half, 2, edge, c),
                coarse_cotangent.reshape(edge, edge, edge, c),
                conv_weight.reshape(27, c, c),
                down_weight.reshape(8, c, c),
            )
        ),
    )
    coarse, ig, conv_total, down_total = pl.pallas_call(
        finish,
        out_shape=shapes,
        in_specs=[hbm] * 4,
        out_specs=(hbm,) * 4,
        scratch_shapes=[pltpu.SemaphoreType.DMA((4 * PIECES,))],
        compiler_params=pltpu.CompilerParams(vmem_limit_bytes=4 * 1024 * 1024),
    )(*parts)
    return (
        coarse.reshape(1, 1, edge, edge, edge, c),
        ig.reshape(1, 1, edge, edge, edge, c),
        conv_total.reshape(3, 3, 3, c, c),
        down_total.reshape(2, 2, 2, c, c),
    )


def solution(mesh):
    in_specs = (
        P("dp", "region", None, None, None, None),
        P(),
        P(),
        P("dp", "region", None, None, None, None),
        P("dp", "region", None),
        P("dp", "region", None),
        P("dp", "region"),
    )
    out_specs = (
        P("dp", "region", None, None, None, None),
        P("dp", "region", None, None, None, None),
        P(),
        P(),
    )
    return jax.shard_map(local, mesh=mesh, in_specs=in_specs, out_specs=out_specs, check_vma=False)
```

```python
import functools

import jax
import jax.numpy as jnp
from jax import lax
from jax.experimental import pallas as pl
from jax.experimental.pallas import tpu as pltpu
from jax.sharding import PartitionSpec as P

loss_scale = 1024.0
MESH = pl.DeviceIdType.MESH
F32, BF16 = jnp.float32, jnp.bfloat16
PIECES = 1


def nn(a, b):
    return lax.dot_general(a, b, (((1,), (0,)), ((), ())), preferred_element_type=F32)


def nt(a, b):
    return lax.dot_general(a, b, (((1,), (1,)), ((), ())), preferred_element_type=F32)


def shifted(s, low, mid, high):
    edge = s.shape[-2]
    axis = s.ndim - 2
    row = lax.broadcasted_iota(jnp.int32, s.shape, axis)
    first = pltpu.roll(s, 1, axis) * jnp.where(row == 0, low, mid)
    last = pltpu.roll(s, edge - 1, axis) * jnp.where(row == edge - 1, high, mid)
    return first, s * mid, last


def put_plane(dst, x, even, odd, low, mid, high):
    half, c = even.shape[0], even.shape[-1]
    for k, v in enumerate(shifted(even, low, mid, high)):
        dst[x, 0:half, :, 2 * k * c + c : 2 * k * c + 2 * c] = v.astype(BF16)
    for k, v in enumerate(shifted(odd, low, mid, high)):
        dst[x, 1 : half + 1, :, 2 * k * c : 2 * k * c + c] = v.astype(BF16)


def put_row(dst, x, y, row, low, mid, high):
    c = row.shape[-1]
    for k, v in enumerate(shifted(row, low, mid, high)):
        at = 2 * k * c + (y % 2) * c
        dst[x, y // 2, :, at : at + c] = v.astype(BF16)


def masks(nb, a):
    def m(b, c):
        i = (a + 1) * 9 + (b + 1) * 3 + (c + 1)
        i = i - 1 if i > 13 else i
        return jnp.where(nb[i] >= 0, 1.0, 0.0).astype(F32)

    return {b: (m(b, -1), m(b, 0), m(b, 1)) for b in (-1, 0, 1)}


def put_halo(dst, x, even, odd, mask):
    half, edge = even.shape[0], dst.shape[0]
    put_plane(dst, x, even, odd, *mask[0])
    put_row(dst, x, 0, odd[half - 1], *mask[-1])
    put_row(dst, x, edge - 1, even[0], *mask[1])


def zero_rows(dst, edge, c):
    z = jnp.zeros((edge, dst.shape[2], c), BF16)
    for k in range(3):
        dst[1 : edge + 1, 0, :, 2 * k * c : 2 * k * c + c] = z
        dst[1 : edge + 1, edge // 2, :, 2 * k * c + c : 2 * k * c + 2 * c] = z


def tap_of(s, pin, pout):
    b = 2 * s + pin - pout
    return b if 0 <= b <= 2 else None


class Reduction:
    def __init__(self, env, acc, whole, start, n, split, refs):
        self.env, self.acc, self.whole, self.start, self.n = env, acc, whole, start, n
        self.send, self.recv, self.by_z, self.gathered = refs[:4]
        self.h = n // 2
        self.p = self.h // env.dps
        self.half = start + env.core * self.h
        self.piece = self.half + env.dp * self.p
        self.split = split
        if split:
            self.to_core, self.from_core, self.to_dp, self.parts, self.to_z, self.z_all = refs[4:]
            self.s = self.p // env.zs
            steps = (self.core_reduce, self.dp_reduce, self.z_reduce, self.z_gather)
        else:
            self.to_plane, self.parts = refs[4:]
            steps = (self.plane_reduce, self.z_exchange)
        self.steps = steps + (self.dp_gather, self.core_gather)
        self.stage = 0
        self.wait = None

    def go(self, src, dst, peers):
        send, recv = self.send.at[0], self.recv.at[self.stage]
        for k, to in enumerate(peers, 1):
            self.env.send(src(k), dst.at[k], send, recv, to)
        self.wait = (dst.at[pl.ds(1, len(peers))], send, recv)

    def swap(self, src, dst):
        send, recv = self.send.at[0], self.recv.at[self.stage]
        self.env.send(src, dst, send, recv, self.env.mate)
        self.wait = (dst, send, recv)

    def land(self):
        size, send, recv = self.wait
        copy = pltpu.make_async_remote_copy(
            src_ref=size, dst_ref=size, send_sem=send, recv_sem=recv,
            device_id=self.env.mate, device_id_type=MESH,
        )
        copy.wait()

    def step(self):
        if self.stage > 0:
            self.land()
        if self.stage < len(self.steps):
            self.steps[self.stage]()
        self.stage += 1

    def done(self):
        return self.stage > len(self.steps)

    def core_reduce(self):
        other = self.start + (1 - self.env.core) * self.h
        self.to_core[...] = self.acc[rows_at(other, self.h)].astype(BF16)
        self.swap(self.to_core, self.from_core)

    def dp_reduce(self):
        env, p = self.env, self.p
        part = self.acc[rows_at(self.half, self.h)] + self.from_core[...].astype(F32)
        self.acc[rows_at(self.half, self.h)] = part
        self.to_dp[...] = part.astype(BF16)
        self.go(lambda k: self.to_dp.at[rows_at(env.dp_at(k) * p, p)], self.parts, env.dp_peers)

    def plane_sum(self):
        part = self.acc[rows_at(self.piece, self.p)]
        for k in range(1, self.parts.shape[0]):
            part += self.parts[k].astype(F32)
        return part

    def plane_reduce(self):
        env, h, p = self.env, self.h, self.p
        self.to_plane[...] = self.acc[pl.ds(self.start, self.n)].astype(BF16)

        def piece(k):
            dp, core = env.plane_at(k)
            return self.to_plane.at[rows_at(core * h + dp * p, p)]

        self.go(piece, self.parts, env.plane_peers)

    def z_exchange(self):
        self.by_z[0] = self.plane_sum().astype(BF16)
        self.go(lambda k: self.by_z.at[0], self.by_z, self.env.z_peers)

    def z_reduce(self):
        env, s = self.env, self.s
        part = self.plane_sum()
        self.acc[rows_at(self.piece, self.p)] = part
        self.to_z[...] = part.astype(BF16)
        self.go(lambda k: self.to_z.at[rows_at(env.z_at(k) * s, s)], self.by_z, env.z_peers)

    def z_gather(self):
        env = self.env
        part = self.acc[rows_at(self.piece + env.z * self.s, self.s)]
        for k in range(1, env.zs):
            part += self.by_z[k].astype(F32)
        self.z_all[0] = part.astype(BF16)
        self.go(lambda k: self.z_all.at[0], self.z_all, env.z_peers)

    def dp_gather(self):
        env = self.env
        if self.split:
            for k in range(env.zs):
                row = lax.rem(env.z - k + env.zs, env.zs) * self.s
                self.gathered[0, rows_at(row, self.s)] = self.z_all[k]
        else:
            part = self.by_z[env.z].astype(F32)
            for z in range(1, env.zs):
                part += self.by_z[lax.rem(env.z - z + env.zs, env.zs)].astype(F32)
            self.gathered[0] = part.astype(BF16)
        self.go(lambda k: self.gathered.at[0], self.gathered, env.dp_peers)

    def core_gather(self):
        env, p = self.env, self.p
        for k in range(env.dps):
            row = lax.rem(env.dp - k + env.dps, env.dps) * p
            self.whole[rows_at(self.half + row, p)] = self.gathered[k]
        ref = self.whole.at[rows_at(self.half, self.h)]
        self.swap(ref, ref)


def reduction_scratch(n, split, dps, zs, c):
    h = n // 2
    p = h // dps
    s = p // zs if split else p
    out = [
        pltpu.SemaphoreType.DMA((1,)),
        pltpu.SemaphoreType.DMA((6 if split else 4,)),
        pltpu.VMEM((zs, s, c), BF16),
        pltpu.VMEM((dps, p, c), BF16),
    ]
    if split:
        out += [pltpu.VMEM((h, c), BF16)] * 3
        out += [pltpu.VMEM((dps, p, c), BF16)]
        out += [pltpu.VMEM((p, c), BF16), pltpu.VMEM((zs, s, c), BF16)]
    else:
        out += [pltpu.VMEM((n, c), BF16), pltpu.VMEM((2 * dps, p, c), BF16)]
    return out


def rows_at(start, n):
    return pl.ds(pl.multiple_of(start, 16) if not isinstance(start, int) else start, n)


class Peers:
    def __init__(self, dps, zs):
        self.dps, self.zs = dps, zs
        n = 2 * zs
        self.dp, self.region = lax.axis_index("dp"), lax.axis_index("region")
        self.core, self.z = lax.rem(self.region, 2), lax.div(self.region, 2)
        self.mate = (self.dp, self.region + 1 - 2 * self.core)
        self.right = (self.dp, lax.rem(self.region + 1, n))
        self.left = (self.dp, lax.rem(self.region + n - 1, n))
        self.dp_peers = [(self.dp_at(k), self.region) for k in range(1, dps)]
        self.z_peers = [(self.dp, 2 * self.z_at(k) + self.core) for k in range(1, zs)]
        self.plane_peers = []
        for k in range(1, 2 * dps):
            dp, core = self.plane_at(k)
            self.plane_peers.append((dp, 2 * self.z + core))
        self.peers = [self.right, self.left] + self.plane_peers + self.z_peers

    def plane_at(self, k):
        rank = lax.rem(2 * self.dp + self.core + k, 2 * self.dps)
        return lax.div(rank, 2), lax.rem(rank, 2)

    def dp_at(self, k):
        return lax.rem(self.dp + k, self.dps)

    def z_at(self, k):
        return lax.rem(self.z + k, self.zs)

    def greet(self):
        barrier = pltpu.get_barrier_semaphore()
        for peer in self.peers:
            pl.semaphore_signal(barrier, inc=1, device_id=peer, device_id_type=MESH)

    def met(self):
        pl.semaphore_wait(pltpu.get_barrier_semaphore(), len(self.peers))

    def send(self, src, dst, send, recv, to):
        copy = pltpu.make_async_remote_copy(
            src_ref=src, dst_ref=dst, send_sem=send, recv_sem=recv,
            device_id=to, device_id_type=MESH,
        )
        copy.start()
        return copy


def start(src, dst, sem):
    copy = pltpu.make_async_copy(src, dst, sem)
    copy.start()
    return copy


def kernel(
    sizes, nb_hbm, xyz_hbm, parent, f_hbm, cot, cw_hbm, dw_hbm,
    coarse_out, ig, conv_out, down_out,
    f, cw, dw, field, wide, gfold, up, outf, gt, tt, acc, whole,
    flo, fhi, cot1, cot2, tag, tag2, ch, clo, chi, blocks, blocks2, nb, xyz, sends, recvs, loads, *refs
):
    dps, zs, cuts, conv_rows, down_rows = sizes
    env = Peers(dps, zs)
    edge, c = f.shape[0], f.shape[-1]
    half = edge // 2
    rows = half * edge
    live = {}
    at = used = 0
    for k, (size, split) in enumerate(cuts):
        if size:
            count = 10 if split else 6
            live[k] = Reduction(env, acc, whole, at, size, split, refs[used : used + count])
            used += count
        at += size
    down_at = len(cuts) - 1

    def advance(*which):
        for k in which:
            if k in live and not live[k].done():
                live[k].step()

    def send(i, src, dst, to):
        return env.send(src, dst, sends.at[i], recvs.at[i], to)

    step = 4
    laps = edge // step
    parts = [pl.ds(i * step, step) for i in range(laps)]
    f_copies = [start(f_hbm.at[p], f.at[p], loads.at[2 + i]) for i, p in enumerate(parts)]
    env.greet()
    small = (nb_hbm, nb), (xyz_hbm, xyz)
    small_copies = [start(a, b, loads.at[i]) for i, (a, b) in enumerate(small)]
    cw_copy = start(cw_hbm, cw, loads.at[laps + 2])
    mine_at = pl.ds(env.core * half, half)

    def window(x, m, a, s):
        return field[pl.ds(x + a, m), s : s + half].reshape(m * rows, 6 * c)

    def lhs(x, m):
        return jnp.concatenate([window(x, m, a, s) for a in range(3) for s in range(2)], -1)

    zero_rows(field, edge, c)

    for i, copy in enumerate(f_copies):
        copy.wait()
        if i == laps - 1:
            cot1_copy = start(cot.at[mine_at], cot1, loads.at[laps + 3])
            dw_copy = start(dw_hbm, dw, loads.at[laps + 4])

        @pl.loop(i * step, (i + 1) * step)
        def _(x):
            put_plane(
                field, x + 1, f[x, :, 0].astype(F32), f[x, :, 1].astype(F32), 0.0, 1.0, 0.0
            )

    env.met()
    theirs_at = pl.ds((1 - env.core) * half, half)
    last = 2 * zs - 1

    def shift(i, src, dst, to, leaves, comes):
        copy = pltpu.make_async_remote_copy(
            src_ref=src, dst_ref=dst, send_sem=sends.at[i], recv_sem=recvs.at[i],
            device_id=to, device_id_type=MESH,
        )

        @pl.when(leaves)
        def _():
            copy.start()

        @pl.when(jnp.logical_not(comes))
        def _():
            dst[...] = jnp.zeros_like(dst)

        return copy, leaves, comes

    def settle(copy, leaves, comes):
        @pl.when(leaves)
        def _():
            copy.wait_send()

        @pl.when(comes)
        def _():
            copy.wait_recv()

    has_right, has_left = env.region < last, env.region > 0
    up_copy = shift(2, f.at[edge - 1], flo, env.right, has_right, has_left)
    down_copy = shift(3, f.at[0], fhi, env.left, has_left, has_right)
    cot_copy = send(0, cot.at[theirs_at], cot2, env.mate)

    zero = jnp.zeros((c, c), BF16)

    def weights(block):
        for a in range(3):
            for s in range(2):
                for k in range(3):
                    for pin in range(2):
                        at = ((2 * a + s) * 3 + k) * 2 * c + pin * c
                        for pout in range(2):
                            b = tap_of(s, pin, pout)
                            wide[at : at + c, pout * c : (pout + 1) * c] = (
                                zero if b is None else block(a, b, k)
                            )

    cw_copy.wait()
    weights(lambda a, b, k: cw[9 * a + 3 * b + k])
    origin = lax.div(env.dp, dps)

    def forward(m, to, scale=1):
        @pl.loop(origin + m, origin + to)
        def _(i):
            x = i * (step * scale)
            out = nn(lhs(x, step), wide[...]).reshape(step, half, edge, 2 * c)
            for q in range(2):
                outf[q, pl.ds(x, step)] = (
                    (out[..., q * c : (q + 1) * c] + f[pl.ds(x, step), :, q].astype(F32))
                    .astype(BF16)
                    .astype(F32)
                )

    forward(1, laps // 2)

    for copy in small_copies:
        copy.wait()
    quad = lax.rem(xyz[1], 2) * 2 + lax.rem(xyz[2], 2)
    octant = env.core * 4 + quad
    tag[...] = jnp.full(tag.shape, parent[0, 0] * 8 + octant, jnp.int32)
    tag_copy = send(1, tag, tag2, env.mate)
    below, above = masks(nb, -1), masks(nb, 1)

    cot1_copy.wait()
    dw_copy.wait()
    cot_copy.wait()
    home = parent[0, 0] == env.region
    picked = jnp.zeros((half, half, half, c), F32)
    for y in range(2):
        at = (slice(None), slice(y * half, (y + 1) * half))
        both = jnp.where(home, cot1[at].astype(F32), cot2[at].astype(F32))
        for z in range(2):
            picked = jnp.where(quad == 2 * y + z, both[:, :, z * half : (z + 1) * half], picked)
    ch[...] = picked.astype(BF16)
    clo_copy = shift(4, ch.at[half - 1], clo, env.right, has_right, has_left)
    chi_copy = shift(5, ch.at[0], chi, env.left, has_left, has_right)

    up[...] = jnp.zeros_like(up)

    def lift(v):
        m = v.shape[0] * v.shape[1]
        v = v.astype(F32).reshape(m, half, c)
        for r in range(2):
            up[r, 0:m, pl.ds(r, half, 2), :] = v
        both = [up[r, 0:m].reshape(m * edge, c).astype(BF16) for r in range(2)]
        return jnp.concatenate(both, -1)

    def dwt(p):
        return jnp.concatenate(
            [jnp.concatenate([dw[4 * p + 2 * q + r] for r in range(2)], -1) for q in range(2)], 0
        )

    raised = lift(picked)
    for p in range(2):
        g = nt(raised, dwt(p)).astype(BF16).reshape(half, half, edge, 2 * c)
        for i in range(half):
            gfold[2 * i + p] = g[i]

    settle(*up_copy)
    settle(*down_copy)
    put_halo(field, 0, flo[:, 0].astype(F32), flo[:, 1].astype(F32), below)
    put_halo(field, edge + 1, fhi[:, 0].astype(F32), fhi[:, 1].astype(F32), above)

    flat = gfold[...].reshape(edge * rows, 2 * c)
    gt[...] = flat.astype(F32).T.astype(BF16)
    if conv_rows > 27 * c:
        acc[27 * c : conv_rows] = jnp.zeros((conv_rows - 27 * c, c), F32)
    if down_rows > 8 * c:
        acc[conv_rows + 8 * c :] = jnp.zeros((down_rows - 8 * c, c), F32)
    def gradient(a):
        for s in range(2):
            tt[s] = nn(gt[...], window(0, edge, a, s))
        for b in range(3):
            for k in range(3):
                total = jnp.zeros((c, c), F32)
                for s in range(2):
                    for pin in range(2):
                        for pout in range(2):
                            if tap_of(s, pin, pout) == b:
                                at = (2 * k + pin) * c
                                total += tt[s, pout * c : (pout + 1) * c, at : at + c]
                tap = 9 * a + 3 * b + k
                acc[tap * c : (tap + 1) * c] = total.T * (1.0 / loss_scale)

    gradient(0)
    advance(0)
    gradient(1)
    advance(1, 0)
    gradient(2)
    advance(2, 1)
    forward(laps // 2, laps - 1)
    advance(0, 2)
    forward(0, 1, laps - 1)
    advance(1)
    forward(1, 2, laps - 1)
    advance(0)

    taken = []
    for p in range(2):
        for r in range(2):
            halves = []
            for q in range(2):
                pieces = [
                    outf[q, 2 * i + p, :, pl.ds(r, half, 2), :].reshape(half * half, c)
                    for i in range(half)
                ]
                halves.append(jnp.concatenate(pieces, 0).astype(BF16))
            taken.append(jnp.concatenate(halves, -1))
    cht = ch[...].reshape(half**3, c).astype(F32).T.astype(BF16)
    for p in range(2):
        for r in range(2):
            d = nn(cht, taken[2 * p + r])
            for q in range(2):
                at = conv_rows + (4 * p + 2 * q + r) * c
                acc[at : at + c] = d[:, q * c : (q + 1) * c].T * (1.0 / loss_scale)
    advance(down_at, 2)
    dwf = jnp.concatenate(
        [dw[4 * p + 2 * q + r] for p in range(2) for r in range(2) for q in range(2)], 0
    )
    blocks[...] = nn(jnp.concatenate(taken, -1), dwf).astype(BF16).reshape(blocks.shape)
    blocks_copy = send(6, blocks, blocks2, env.mate)

    settle(*clo_copy)
    settle(*chi_copy)
    for edge_of, p, x, mask in ((clo, 1, 0, below), (chi, 0, edge + 1, above)):
        g = nt(lift(edge_of[...][None]), dwt(p)).astype(BF16).astype(F32)
        g = g.reshape(half, edge, 2 * c)
        put_halo(field, x, g[..., :c], g[..., c:], mask)
    advance(1)

    @pl.loop(0, edge)
    def _(x):
        g = gfold[x].astype(F32)
        put_plane(field, x + 1, g[..., :c], g[..., c:], 0.0, 1.0, 0.0)

    weights(lambda a, b, k: cw[9 * (2 - a) + 3 * (2 - b) + 2 - k].T)


    def backward(m, to):
        @pl.loop(origin + m, origin + to)
        def _(i):
            x = i * step
            out = nn(lhs(x, step), wide[...]).reshape(step, half, edge, 2 * c)
            out = (out + gfold[pl.ds(x, step)].astype(F32)).astype(BF16)
            for q in range(2):
                ig[pl.ds(x, step), :, q] = out[..., q * c : (q + 1) * c]

    quarter = laps // 4
    backward(0, quarter)
    advance(2, down_at, 0, 1)
    backward(quarter, 2 * quarter)
    advance(2, down_at)
    backward(2 * quarter, 3 * quarter)
    advance(0, 1)
    backward(3 * quarter, laps)
    advance(2)

    tag_copy.wait()
    blocks_copy.wait()
    mine, theirs = blocks[...].astype(F32), blocks2[...].astype(F32)
    own_tag, other_tag = tag[0:1, :], tag2[0:1, :]
    for x in range(2):
        for y in range(2):
            pair = []
            for z in range(2):
                here = env.region * 8 + 4 * x + 2 * y + z
                ours = jnp.where(own_tag == here, 1.0, 0.0).astype(F32)
                others = jnp.where(other_tag == here, 1.0, 0.0).astype(F32)
                pair.append(mine * ours + theirs * others)
            coarse_out[x * half : (x + 1) * half, y * half : (y + 1) * half] = jnp.concatenate(
                pair, 2
            ).astype(BF16)
    def finish_chunk(k):
        one = live[k]
        while not one.done():
            one.step()
        rows = min(one.start + one.n, 27 * c)
        if k != down_at:
            conv_out[one.start : rows] = whole[one.start : rows].astype(F32)

    advance(down_at, 2)
    for k in (0, 1, 2, down_at):
        if k in live:
            finish_chunk(k)
    down_out[...] = whole[conv_rows : conv_rows + 8 * c].astype(F32)


def finish(*refs):
    n = len(refs) // 2
    sems = refs[2 * n]
    copies = []
    for i in range(n):
        m = refs[i].shape[0] // PIECES
        for k in range(PIECES):
            part = pl.ds(k * m, m)
            sem = sems.at[len(copies)]
            copies.append(start(refs[i].at[part], refs[n + i].at[part], sem))
    for copy in copies:
        copy.wait()


def local(features, conv_weight, down_weight, coarse_cotangent, brick_coords, neighbours, parents):
    edge, c = features.shape[2], features.shape[-1]
    half = edge // 2
    dps, regions = lax.axis_size("dp"), lax.axis_size("region")
    zs = regions // 2
    unit, wide = 32 * dps, 32 * dps * zs
    conv_rows = -(-27 * c // wide) * wide
    down_rows = -(-8 * c // unit) * unit
    ends = [0, 9 * c // wide * wide, 18 * c // wide * wide, conv_rows]
    cuts = tuple((ends[i + 1] - ends[i], True) for i in range(3)) + ((down_rows, False),)
    total = conv_rows + down_rows
    hbm = pl.BlockSpec(memory_space=pl.ANY)
    smem = pl.BlockSpec(memory_space=pltpu.SMEM)
    plane = pltpu.VMEM((half, 2, edge, c), BF16)
    cube = pltpu.VMEM((half, half, half, c), BF16)
    layer = pltpu.VMEM((half, half, c), BF16)
    tags = pltpu.VMEM((8, 128), jnp.int32)
    scratch = [
        pltpu.VMEM((edge, half, 2, edge, c), BF16),
        pltpu.VMEM((27, c, c), BF16),
        pltpu.VMEM((8, c, c), BF16),
        pltpu.VMEM((edge + 2, half + 1, edge, 6 * c), BF16),
        pltpu.VMEM((36 * c, 2 * c), BF16),
        pltpu.VMEM((edge, half, edge, 2 * c), BF16),
        pltpu.VMEM((2, half * half, edge, c), F32),
        pltpu.VMEM((2, edge, half, edge, c), F32),
        pltpu.VMEM((2 * c, edge * half * edge), BF16),
        pltpu.VMEM((2, 2 * c, 6 * c), F32),
        pltpu.VMEM((total, c), F32),
        pltpu.VMEM((total, c), BF16),
        plane,
        plane,
        pltpu.VMEM((half, edge, edge, c), BF16),
        pltpu.VMEM((half, edge, edge, c), BF16),
        tags,
        tags,
        cube,
        layer,
        layer,
        cube,
        cube,
        pltpu.SMEM((26,), jnp.int32),
        pltpu.SMEM((3,), jnp.int32),
        pltpu.SemaphoreType.DMA((7,)),
        pltpu.SemaphoreType.DMA((7,)),
        pltpu.SemaphoreType.DMA((edge // 4 + 5,)),
    ]
    for n, split in cuts:
        if n:
            scratch += reduction_scratch(n, split, dps, zs, c)
    shapes = (
        jax.ShapeDtypeStruct((edge, edge, edge, c), BF16),
        jax.ShapeDtypeStruct((edge, half, 2, edge, c), BF16),
        jax.ShapeDtypeStruct((27 * c, c), F32),
        jax.ShapeDtypeStruct((8 * c, c), F32),
    )
    parts = pl.pallas_call(
        functools.partial(kernel, (dps, zs, cuts, conv_rows, down_rows)),
        out_shape=shapes,
        in_specs=[hbm] * 2 + [smem] + [hbm] * 4,
        out_specs=(pl.BlockSpec(memory_space=pltpu.VMEM),) * 4,
        scratch_shapes=scratch,
        compiler_params=pltpu.CompilerParams(
            collective_id=0, has_side_effects=True, vmem_limit_bytes=40 * 1024 * 1024
        ),
    )(
        pltpu.with_memory_space_constraint(neighbours.reshape(26), pltpu.HBM),
        pltpu.with_memory_space_constraint(brick_coords.reshape(3), pltpu.HBM),
        parents,
        *(
            pltpu.with_memory_space_constraint(v, pltpu.HBM)
            for v in (
                features.reshape(edge, half, 2, edge, c),
                coarse_cotangent.reshape(edge, edge, edge, c),
                conv_weight.reshape(27, c, c),
                down_weight.reshape(8, c, c),
            )
        ),
    )
    coarse, ig, conv_total, down_total = pl.pallas_call(
        finish,
        out_shape=shapes,
        in_specs=[hbm] * 4,
        out_specs=(hbm,) * 4,
        scratch_shapes=[pltpu.SemaphoreType.DMA((4 * PIECES,))],
        compiler_params=pltpu.CompilerParams(vmem_limit_bytes=4 * 1024 * 1024),
    )(*parts)
    return (
        coarse.reshape(1, 1, edge, edge, edge, c),
        ig.reshape(1, 1, edge, edge, edge, c),
        conv_total.reshape(3, 3, 3, c, c),
        down_total.reshape(2, 2, 2, c, c),
    )


def solution(mesh):
    in_specs = (
        P("dp", "region", None, None, None, None),
        P(),
        P(),
        P("dp", "region", None, None, None, None),
        P("dp", "region", None),
        P("dp", "region", None),
        P("dp", "region"),
    )
    out_specs = (
        P("dp", "region", None, None, None, None),
        P("dp", "region", None, None, None, None),
        P(),
        P(),
    )
    return jax.shard_map(local, mesh=mesh, in_specs=in_specs, out_specs=out_specs, check_vma=False)
```
